1024 devices in a mesh: lon: 128 (over z, y_lo, core), lat: 8 (over y_hi, x).
Axes of the slice: x: 4, y: 8 (y_hi: 2, y_lo: 4; y = y_hi * 4 + y_lo), z: 16, core: 2. Of those that a mesh axis runs over, the one named last changes fastest.
Arguments:
- adjoint_height: float32 [4096, 16384], P('lat', 'lon'), may hold values from -6 to 6
- depth: float32 [4096, 16384], P('lat', 'lon'), may hold values from 0.1 to 1
- wet: int32 [4096, 16384], P('lat', 'lon'), may hold values 0 or 1
- basis_lat: float32 [32, 4096], P(None, 'lat'), may hold values from -1.5 to 1.5
- basis_lon: float32 [32, 16384], P(None, 'lon'), may hold values from -1.5 to 1.5
- tile_owner: int32 [256, 1024], P('lat', 'lon'), may hold values from 0 to 127, as said below
- tile_patch: int32 [256, 1024], P('lat', 'lon'), may hold values from 0 to 255
- tile_count: int32 [256, 1024], P('lat', 'lon'), may hold values from 1 to 32
- prior_patches: float32 [8, 128, 256, 256], P('lat', 'lon'), may hold values from 0 to 11
- prior_subfaults: float32 [32, 32], replicated, may hold values from -0.4 to 1.7
Outputs:
- adjoint_final: float32 [4096, 16384], P('lat', 'lon')
- source_gradient: float32 [4096, 16384], P('lat', 'lon')
The draws below stay inside these ranges and needn't reach their ends.
Inputs may be any that keep to these rules, and one draw needn't show every extreme that they name: `tile_owner`: within each device's block of tiles no owner is named more than 3 times, and in every latitude band one owner is named exactly 3 times by every device's block.
All inputs are finite; a program needn't handle non-finite values. No bound on the sum of `wet` on one device may be relied on, other than what follows from the above.
Results may differ from the reference program's by a relative error of at most 0.0002.
Values sent between devices are 32-bit elements; how exact they have to be, the bound alone decides.
No kernel may reach another device: no remote copies, remote signals or barrier semaphores. Data moves between devices by JAX's collectives and lax.ppermute only.
A program may use at most 32 MiB of HBM per device.

```python
import math
import jax
import jax.numpy as jnp
from jax import lax

CLAT = 512
CLON = 128
STEPS = 4
TS = 16
SUB = 32
NPATCH = 256
NLAT = 4096
NLON = 16384
CAP = 3
N_LON = 128
N_LAT = 8


def draw_adjoint_height(key, part):
    return jax.random.truncated_normal(key, -6.0, 6.0, (NLAT, NLON), jnp.float32)


def draw_tile_owner(key, part):
    tile_rows = CLAT // TS
    tile_cols = CLON // TS
    tile_total = tile_rows * tile_cols
    lat_devices = NLAT // CLAT
    lon_devices = NLON // CLON
    slot_total = CAP * lon_devices
    key_full, key_heavy, key_device = jax.random.split(key, 3)
    full_owner = jax.random.randint(key_full, (lat_devices,), 0, lon_devices)
    heavy_flags = (jax.random.randint(key_heavy, (lat_devices, lon_devices), 0, 8) == 0).astype(jnp.int32)
    pair_owner = jnp.arange(slot_total, dtype=jnp.int32) // CAP

    def one_block(band_index, strip_index):
        device_key = jax.random.fold_in(jax.random.fold_in(key_device, band_index), strip_index)
        key_noise, key_shuffle = jax.random.split(device_key)
        noise_part = jax.random.randint(key_noise, (slot_total,), 0, 4096)
        scores = noise_part + 8192 * heavy_flags[band_index][pair_owner] + 65536 * (pair_owner == full_owner[band_index]).astype(jnp.int32)
        scores = scores * slot_total + jnp.arange(slot_total, dtype=jnp.int32)
        unused, chosen = lax.top_k(scores, tile_total)
        owners = chosen // CAP
        shuffle = jax.random.permutation(key_shuffle, tile_total)
        return owners[shuffle].reshape(tile_rows, tile_cols)
    inner = jax.vmap(one_block, in_axes=(None, 0))
    blocks = jax.vmap(inner, in_axes=(0, None))(jnp.arange(lat_devices, dtype=jnp.int32), jnp.arange(lon_devices, dtype=jnp.int32))
    return blocks.transpose(0, 2, 1, 3).reshape(lat_devices * tile_rows, lon_devices * tile_cols).astype(jnp.int32)


def draw_prior_patches(key, part):
    lat_devices = NLAT // CLAT
    lon_devices = NLON // CLON
    key_spread = jax.random.fold_in(key, 0)
    index_line = jnp.arange(NPATCH, dtype=jnp.float32)
    distance = (index_line[:, None] - index_line[None, :]) / 6.0
    kernel = jnp.exp(-distance * distance)
    identity = jnp.eye(NPATCH, dtype=jnp.float32)
    shape = (lat_devices, lon_devices, NPATCH, NPATCH)
    spread = jax.random.uniform(key_spread, shape, jnp.float32, 0.5, 1.5)
    return identity + spread * kernel / 6.0


def draw_prior_subfaults(key, part):
    key_main = jax.random.fold_in(key, 0)
    identity = jnp.eye(SUB, dtype=jnp.float32)
    return identity + jax.random.uniform(key_main, (SUB, SUB), jnp.float32, -0.3, 0.3)


def touch_ends(drawn, key, least, high):
    longest = drawn.shape.index(max(drawn.shape))
    spots = []
    for shift in (0, 1):
        where = [jax.random.randint(jax.random.fold_in(key, axis), (), 0, length) for axis, length in enumerate(drawn.shape)]
        where[longest] = (where[longest] + shift) % drawn.shape[longest]
        spots.append(tuple(where))
    return drawn.at[spots[0]].set(least).at[spots[1]].set(high)


def levels(rng, shape, shards, low, high):
    def one(dim, blocks):
        heights = jax.random.uniform(jax.random.fold_in(jax.random.fold_in(rng, 6), dim), (blocks,), jnp.float32, low / len(shards), high / len(shards))
        return jnp.repeat(jnp.exp(heights), shape[dim] // blocks).reshape((-1,) + (1,) * (len(shape) - dim - 1))

    level = one(*shards[0])
    for cut in shards[1:]:
        level = level * one(*cut)
    return level


def gaussian(own_key, extent, width, bound, cuts=(), kind=jnp.bfloat16):
    level = levels(own_key, extent, cuts, -0.22, 0.18) if cuts else 1.0
    array = jax.random.normal(own_key, extent, jnp.float32) * width * level
    return jnp.minimum(jnp.maximum(array, -bound), bound).astype(kind)


def setup_inputs(seed: int = 0) -> dict:
    arg_keys = jax.random.split(jax.random.key(seed), 11)
    adjoint_height = draw_adjoint_height(jax.random.fold_in(arg_keys[10], 71), 0)
    depth = jnp.clip(jnp.exp(math.log(1.0) - 2.3025851 * jax.random.uniform(arg_keys[1], (NLAT, NLON), jnp.float32) ** levels(arg_keys[1], (NLAT, NLON), ((0, 8), (1, 128)), -0.2, 0.2)), 0.1, 1.0)
    wet = touch_ends((jax.random.randint(arg_keys[2], (NLAT, NLON), 0, 20) < 17).astype(jnp.int32), jax.random.fold_in(arg_keys[2], 1), 0, 1)
    basis_lat = gaussian(arg_keys[3], (SUB, NLAT), 0.25, 1.5, ((1, 8),), jnp.float32)
    basis_lon = gaussian(arg_keys[4], (SUB, NLON), 0.25, 1.5, ((1, 128),), jnp.float32)
    tile_owner = draw_tile_owner(jax.random.fold_in(arg_keys[10], 71), 0)
    tile_patch = touch_ends(jax.random.randint(arg_keys[6], (NLAT // TS, NLON // TS), 0, NPATCH), jax.random.fold_in(arg_keys[6], 1), 0, NPATCH - 1).astype(jnp.int32)
    tile_count = touch_ends(jax.random.randint(arg_keys[7], (NLAT // TS, NLON // TS), 1, SUB + 1), jax.random.fold_in(arg_keys[7], 1), 1, SUB).astype(jnp.int32)
    prior_patches = draw_prior_patches(jax.random.fold_in(arg_keys[10], 71), 0)
    prior_subfaults = draw_prior_subfaults(jax.random.fold_in(arg_keys[10], 71), 0)
    return {"adjoint_height": adjoint_height, "depth": depth, "wet": wet, "basis_lat": basis_lat, "basis_lon": basis_lon, "tile_owner": tile_owner, "tile_patch": tile_patch, "tile_count": tile_count, "prior_patches": prior_patches, "prior_subfaults": prior_subfaults}


COURANT = 0.6


def adjoint_step(height, east, north, wet_depth):
    east_new = east[:, :-1] + COURANT * jnp.minimum(wet_depth[:, :-1], wet_depth[:, 1:]) * (height[:, 1:] - height[:, :-1])
    north_new = north[:-1, :] + COURANT * jnp.minimum(wet_depth[:-1, :], wet_depth[1:, :]) * (height[1:, :] - height[:-1, :])
    height_new = height[1:-1, 1:-1] + COURANT * (east_new[1:-1, 1:] - east_new[1:-1, :-1]) + COURANT * (north_new[1:, 1:-1] - north_new[:-1, 1:-1])
    return height_new, east_new[1:-1, 1:], north_new[1:, 1:-1]


def extend(field):
    looped = jnp.concatenate([field[:, -1:], field, field[:, :1]], axis=1)
    return jnp.pad(looped, ((1, 1), (0, 0)))


def reference(adjoint_height, depth, wet, basis_lat, basis_lon, tile_owner, tile_patch, tile_count, prior_patches, prior_subfaults):
    highest = lax.Precision.HIGHEST
    wet_depth = depth * wet.astype(jnp.float32)
    depth_rim = extend(wet_depth)
    height = adjoint_height
    east = jnp.zeros_like(adjoint_height)
    north = jnp.zeros_like(adjoint_height)
    for repeat in range(STEPS):
        height, east, north = adjoint_step(extend(height), extend(east), extend(north), depth_rim)
    tile_rows = NLAT // TS
    tile_cols = NLON // TS
    lat_basis = basis_lat.reshape(SUB, tile_rows, TS).transpose(1, 0, 2)
    lon_basis = basis_lon.reshape(SUB, tile_cols, TS)
    blocks = height.reshape(tile_rows, TS, tile_cols, TS)

    def tile_row(pair):
        block, row_basis = pair
        partial_value = jnp.einsum('aib,sib->sai', block, lon_basis, precision=highest)
        return jnp.einsum('sa,sai->is', row_basis, partial_value, precision=highest)

    sensitivity = lax.map(tile_row, (blocks, lat_basis))
    active = (jnp.arange(SUB)[None, None, :] < tile_count[:, :, None]).astype(jnp.float32)
    sensitivity = sensitivity * active
    band_index = (jnp.arange(tile_rows) // (CLAT // TS)).astype(jnp.int32)
    group_index = (band_index[:, None] * N_LON + tile_owner) * NPATCH + tile_patch
    parameters = jax.ops.segment_sum(sensitivity.reshape(-1, SUB), group_index.reshape(-1), num_segments=N_LAT * N_LON * NPATCH)
    parameters = parameters.reshape(N_LAT, N_LON, NPATCH, SUB)
    mixed = jnp.einsum('lomn,lons->loms', prior_patches, parameters, precision=highest)
    smoothed = jnp.einsum('loms,st->lomt', mixed, prior_subfaults, precision=highest)
    tile_value = smoothed.reshape(-1, SUB)[group_index] * active

    def gradient_row(pair):
        row_basis, row_value = pair
        weighted = row_basis[:, :, None] * row_value.T[:, None, :]
        return jnp.einsum('sai,sib->aib', weighted, lon_basis, precision=highest)

    gradient = lax.map(gradient_row, (lat_basis, tile_value)).reshape(NLAT, NLON)
    return height, gradient
```

```python
import jax
import jax.numpy as jnp
from jax import lax
from jax.experimental import pallas as pl
from jax.experimental.pallas import tpu as pltpu
from jax.sharding import PartitionSpec as P

STEPS = 4
RIM = 4
TS = 16
SUB = 32
NPATCH = 256
CAP = 3
COURANT = 0.6
LANES = 128
F32 = jnp.float32
BF16 = jnp.bfloat16


def iota(shape, dim):
    return lax.broadcasted_iota(jnp.int32, shape, dim)


def parts(x):
    high = x.astype(BF16)
    return high, (x - high.astype(F32)).astype(BF16)


def dot(a, b):
    return lax.dot_general(a, b, (((1,), (0,)), ((), ())), preferred_element_type=F32)


def dot_t(a, b):
    return lax.dot_general(a, b, (((1,), (1,)), ((), ())), preferred_element_type=F32)


def one_hot_dot(hot, x):
    high, low = parts(x)
    return dot(hot, high) + dot(hot, low)


def dot3(a, b, product=dot):
    a_high, a_low = parts(a)
    b_high, b_low = parts(b)
    return product(a_high, b_high) + (product(a_high, b_low) + product(a_low, b_high))


def spread_lon(basis_lon):
    tiles = LANES // TS
    tall = jnp.concatenate([basis_lon] * tiles, axis=0)
    inside = iota(tall.shape, 0) // SUB == iota(tall.shape, 1) // TS
    return jnp.where(inside, tall, 0.0)


def edge_columns(height, wet_depth):
    lane = iota(height.shape, 1)
    near = jnp.where(lane < RIM, height, pltpu.roll(wet_depth, RIM, 1))
    far = jnp.where(lane >= LANES - RIM, height, pltpu.roll(wet_depth, LANES - RIM, 1))
    return jnp.where(lane < LANES // 2, near, far)


def prepare(h_ref, d_ref, w_ref, lat_ref, owner_ref, patch_ref, count_ref,
            edge_ref, lat4_ref, hot_ref, hot_t_ref, mask_ref):
    height = h_ref[...]
    wet_depth = d_ref[...] * w_ref[...].astype(F32)
    edges = edge_columns(height, wet_depth).T
    edge_ref[0:8, :] = edges[0:8]
    edge_ref[8:16, :] = edges[LANES - 8:LANES]
    lat4_ref[...] = jnp.concatenate([lat_ref[...]] * 4, axis=0).T

    def column(ref):
        table = ref[...].astype(F32)
        flat = jnp.concatenate([table[:, k:k + 1] for k in range(table.shape[1])], axis=0)
        return jnp.broadcast_to(flat, (flat.shape[0], LANES))

    owner = column(owner_ref)
    patch = column(patch_ref)
    count = column(count_ref)
    owner_row = owner.T
    total = owner.shape[0]
    hot_t_ref[...] = (owner == iota(owner.shape, 1).astype(F32)).astype(BF16)
    hot_ref[...] = (owner_row == iota(owner_row.shape, 0).astype(F32)).astype(BF16)
    rank = jnp.zeros((total, LANES), F32)
    for q in range(total // LANES):
        row = jnp.broadcast_to(owner_row[0:1, q * LANES:(q + 1) * LANES], (total, LANES))
        earlier = iota((total, LANES), 1) + q * LANES < iota((total, LANES), 0)
        rank = rank + jnp.where(earlier & (row == owner), 1.0, 0.0)
    rank = jnp.broadcast_to(jnp.sum(rank, axis=1, keepdims=True), (total, LANES))
    lane = iota((total, LANES), 1)
    group = (lane // SUB).astype(F32)
    place = (lane % SUB).astype(F32)
    live = jnp.where((rank == group) & (place < count), 1.0, 0.0)
    number = jnp.where(rank == place, patch, 0.0)
    mask_ref[...] = jnp.where(lane < CAP * SUB, live, number)


def rims(parity_lat, ra, rb):
    south = jnp.where(parity_lat == 0, ra, rb)
    north = jnp.where(parity_lat == 0, rb, ra)
    return north, south


def corners(par_ref, edge_ref, ra_ref, rb_ref, first_ref, second_ref, east_ref, west_ref):
    north, south = rims(par_ref[1], ra_ref[...], rb_ref[...])
    row = iota((8, LANES), 0)
    top = edge_columns(south, pltpu.roll(south, 4, 0))
    low = edge_columns(pltpu.roll(north, 4, 0), north)
    block = jnp.concatenate(
        [jnp.where(row < 4, top, 0.0), jnp.zeros((LANES - 16, LANES), F32), jnp.where(row < 4, 0.0, low)],
        axis=0,
    ).T
    west = jnp.concatenate([edge_ref[0:8, :], block[0:8]], axis=1)
    east = jnp.concatenate([edge_ref[8:16, :], block[LANES - 8:LANES]], axis=1)
    west_ref[...] = west
    east_ref[...] = east
    first_ref[...] = jnp.where(par_ref[0] == 0, east, west)
    second_ref[...] = jnp.where(par_ref[0] == 0, west, east)


def flux_update(height, east, north, ce, cn, right, below):
    east = east + ce * (right - height)
    north = north + cn * (below - height)
    return east, north


def strip(height, wet_depth):
    rows, lanes = height.shape
    ce = COURANT * jnp.minimum(wet_depth, pltpu.roll(wet_depth, rows - 1, 0))
    cn = COURANT * jnp.minimum(wet_depth, pltpu.roll(wet_depth, lanes - 1, 1))
    east = jnp.zeros_like(height)
    north = jnp.zeros_like(height)
    heights, easts = [height], []
    for _ in range(STEPS):
        east, north = flux_update(
            height, east, north, ce, cn, pltpu.roll(height, rows - 1, 0), pltpu.roll(height, lanes - 1, 1)
        )
        height = (
            height
            + COURANT * (east - pltpu.roll(east, 1, 0))
            + COURANT * (north - pltpu.roll(north, 1, 1))
        )
        heights.append(height)
        easts.append(east)
    return heights, easts


def forward(par_ref, h_ref, d_ref, w_ref, na_ref, nb_ref, east_ref, west_ref, ea_ref, eb_ref,
            lon_ref, lat4_ref, hot_ref, mask_ref, out_ref, send_ref):
    rows_own = h_ref.shape[0]
    north_rim, south_rim = rims(par_ref[1], na_ref[...], nb_ref[...])
    from_east = jnp.where(par_ref[0] == 0, ea_ref[...], eb_ref[...])
    from_west = jnp.where(par_ref[0] == 0, eb_ref[...], ea_ref[...])
    own_west, own_east = west_ref[...], east_ref[...]
    west_h = jnp.concatenate([from_west[4:8], own_west[0:4]], axis=0)
    west_d = jnp.concatenate([from_west[0:4], own_west[4:8]], axis=0)
    east_h = jnp.concatenate([own_east[4:8], from_east[0:4]], axis=0)
    east_d = jnp.concatenate([own_east[0:4], from_east[4:8]], axis=0)
    _, west_easts = strip(west_h, west_d)
    east_heights, _ = strip(east_h, east_d)
    lines = [e[3:4] for e in west_easts] + [x[4:5] for x in east_heights[:STEPS]] + [east_d[4:5]]
    lines.append(jnp.zeros((LANES - len(lines), lines[0].shape[1]), F32))
    table = jnp.concatenate(lines, axis=0).T
    table = jnp.concatenate([table[rows_own + LANES - 8:], table[:rows_own + 8]], axis=0)

    row8 = iota((8, LANES), 0)
    height = jnp.concatenate(
        [
            jnp.where(row8 < 4, 0.0, pltpu.roll(north_rim, 4, 0)),
            h_ref[...],
            jnp.where(row8 < 4, south_rim, 0.0),
        ],
        axis=0,
    )
    wet_depth = jnp.concatenate(
        [
            jnp.where(row8 < 4, 0.0, north_rim),
            d_ref[...] * w_ref[...].astype(F32),
            jnp.where(row8 < 4, pltpu.roll(south_rim, 4, 0), 0.0),
        ],
        axis=0,
    )
    rows = height.shape[0]
    lane = iota(height.shape, 1)

    def line(index):
        return jnp.broadcast_to(table[:, index:index + 1], height.shape)

    def right_of(field, index):
        return jnp.where(lane == LANES - 1, line(index), pltpu.roll(field, LANES - 1, 1))

    ce = COURANT * jnp.minimum(wet_depth, right_of(wet_depth, 2 * STEPS))
    cn = COURANT * jnp.minimum(wet_depth, pltpu.roll(wet_depth, rows - 1, 0))
    east = jnp.zeros_like(height)
    north = jnp.zeros_like(height)
    for k in range(STEPS):
        east, north = flux_update(
            height, east, north, ce, cn, right_of(height, STEPS + k), pltpu.roll(height, rows - 1, 0)
        )
        before = jnp.where(lane == 0, line(k), pltpu.roll(east, 1, 1))
        height = height + COURANT * (east - before) + COURANT * (north - pltpu.roll(north, 1, 0))
    final = height[8:8 + rows_own]
    out_ref[...] = final

    product = dot3(final, spread_lon(lon_ref[...]), dot_t)
    lat4 = lat4_ref[...]
    product = product * jnp.concatenate([lat4, lat4], axis=1)
    tile_rows = rows_own // TS
    sums = jnp.sum(product.reshape(tile_rows, TS, product.shape[1]), axis=1)
    group = iota((tile_rows, LANES), 1) // SUB
    stacked = []
    for q in range(sums.shape[1] // LANES):
        for g in range(4):
            own = jnp.where(group == g, sums[:, q * LANES:(q + 1) * LANES], 0.0)
            own = own + pltpu.roll(own, 2 * SUB, 1)
            stacked.append(own + pltpu.roll(own, SUB, 1))
    values = jnp.concatenate(stacked, axis=0)
    mask = mask_ref[...]
    filled = jnp.where(iota(mask.shape, 1) < CAP * SUB, values * mask, mask)
    send_ref[...] = one_hot_dot(hot_ref[...], filled)


def smooth(recv_ref, prior_ref, sub_ref, reply_ref):
    received = recv_ref[...]
    turned = received.T
    devices = received.shape[0]
    group = iota((devices, LANES), 1) // SUB
    gathered = jnp.zeros((NPATCH, LANES), F32)
    for r in range(CAP):
        line = jnp.broadcast_to(turned[CAP * SUB + r:CAP * SUB + r + 1], (NPATCH, devices))
        member = (line == iota((NPATCH, devices), 0).astype(F32)).astype(BF16)
        gathered = gathered + one_hot_dot(member, jnp.where(group == r, received, 0.0))
    mixed = dot3(prior_ref[...], gathered)
    sub = jnp.concatenate([sub_ref[...]] * 4, axis=1)
    sub = jnp.concatenate([sub] * CAP + [jnp.zeros_like(sub)], axis=0)
    smoothed = dot3(mixed, sub)
    group = iota(smoothed.shape, 1) // SUB
    reply = jnp.zeros((devices, LANES), F32)
    for r in range(CAP):
        line = jnp.broadcast_to(received[:, CAP * SUB + r:CAP * SUB + r + 1], (devices, NPATCH))
        member = (line == iota((devices, NPATCH), 1).astype(F32)).astype(BF16)
        reply = reply + one_hot_dot(member, jnp.where(group == r, smoothed, 0.0))
    reply_ref[...] = reply


def backward(ret_ref, hot_t_ref, mask_ref, lat4_ref, lon_ref, out_ref):
    mask = mask_ref[...]
    picked = one_hot_dot(hot_t_ref[...], ret_ref[...])
    picked = jnp.where(iota(mask.shape, 1) < CAP * SUB, picked * mask, 0.0)
    picked = picked + pltpu.roll(picked, 2 * SUB, 1)
    picked = picked + pltpu.roll(picked, SUB, 1)
    tile_rows = out_ref.shape[0] // TS
    group = iota((tile_rows, LANES), 1) // SUB
    halves = []
    for q in range(2):
        half = picked[4 * q * tile_rows:(4 * q + 1) * tile_rows]
        for g in range(1, 4):
            block = picked[(4 * q + g) * tile_rows:(4 * q + g + 1) * tile_rows]
            half = jnp.where(group == g, block, half)
        halves.append(half)
    value = jnp.concatenate(halves, axis=1)
    wide = jnp.broadcast_to(value[:, None, :], (tile_rows, TS, value.shape[1])).reshape(
        out_ref.shape[0], value.shape[1]
    )
    lat4 = lat4_ref[...]
    weighted = wide * jnp.concatenate([lat4, lat4], axis=1)
    out_ref[...] = dot3(weighted, spread_lon(lon_ref[...]))


VMEM = pl.BlockSpec(memory_space=pltpu.VMEM)
SMEM = pl.BlockSpec(memory_space=pltpu.SMEM)


def call(kernel, outs, *args, scalars=0):
    return pl.pallas_call(
        kernel,
        out_shape=[jax.ShapeDtypeStruct(shape, dtype) for shape, dtype in outs],
        in_specs=[SMEM] * scalars + [VMEM] * (len(args) - scalars),
        out_specs=[VMEM] * len(outs),
        compiler_params=pltpu.CompilerParams(vmem_limit_bytes=32 * 1024 * 1024),
    )(*args)


def swap_pairs(axis, first, periodic):
    count = lax.axis_size(axis)
    pairs = []
    for a in range(first, count, 2):
        b = a + 1
        if b == count:
            if not periodic:
                continue
            b = 0
        pairs += [(a, b), (b, a)]
    return pairs


def swap(payload, axis, periodic):
    return [
        lax.ppermute(x, axis, swap_pairs(axis, first, periodic)) for first, x in enumerate(payload)
    ]


def local(
    adjoint_height,
    depth,
    wet,
    basis_lat,
    basis_lon,
    tile_owner,
    tile_patch,
    tile_count,
    prior_patches,
    prior_subfaults,
):
    rows, cols = adjoint_height.shape
    lon_devices = lax.axis_size("lon")
    total = (rows // TS) * (cols // TS)
    parity = jnp.stack([lax.axis_index("lon") % 2, lax.axis_index("lat") % 2]).astype(jnp.int32)

    def edge_rows(start):
        def cut(x):
            return lax.dynamic_slice_in_dim(x, start, RIM, axis=0)
        return jnp.concatenate([cut(adjoint_height), cut(depth) * cut(wet).astype(F32)], axis=0)

    last = rows - RIM
    a_rows = edge_rows(jnp.where(parity[1] == 0, last, 0))
    b_rows = edge_rows(jnp.where(parity[1] == 0, 0, last))
    north_a, north_b = swap([a_rows, b_rows], "lat", False)
    edges, lat4, hot, hot_t, mask = call(
        prepare,
        [
            ((16, rows), F32),
            ((rows, LANES), F32),
            ((lon_devices, total), BF16),
            ((total, lon_devices), BF16),
            ((total, LANES), F32),
        ],
        adjoint_height, depth, wet, basis_lat, tile_owner, tile_patch, tile_count,
    )
    wide = ((8, rows + LANES), F32)
    first, second, east, west = call(
        corners, [wide] * 4, parity, edges, north_a, north_b, scalars=1
    )
    east_a, east_b = swap([first, second], "lon", True)
    final, sent = call(
        forward,
        [((rows, cols), F32), ((lon_devices, LANES), F32)],
        parity, adjoint_height, depth, wet, north_a, north_b, east, west, east_a, east_b,
        basis_lon, lat4, hot, mask,
        scalars=1,
    )
    received = lax.all_to_all(sent, "lon", split_axis=0, concat_axis=0, tiled=True)
    (replies,) = call(
        smooth,
        [((lon_devices, LANES), F32)],
        received, prior_patches.reshape(NPATCH, NPATCH), prior_subfaults,
    )
    returned = lax.all_to_all(replies, "lon", split_axis=0, concat_axis=0, tiled=True)
    (gradient,) = call(
        backward, [((rows, cols), F32)], returned, hot_t, mask, lat4, basis_lon
    )
    return (final, gradient)


def solution(mesh):
    return jax.shard_map(
        local,
        mesh=mesh,
        in_specs=(
            P("lat", "lon"),
            P("lat", "lon"),
            P("lat", "lon"),
            P(None, "lat"),
            P(None, "lon"),
            P("lat", "lon"),
            P("lat", "lon"),
            P("lat", "lon"),
            P("lat", "lon", None, None),
            P(),
        ),
        out_specs=(P("lat", "lon"), P("lat", "lon")),
        check_vma=False,
    )
```

```python
import jax
import jax.numpy as jnp
from jax import lax
from jax.experimental import pallas as pl
from jax.experimental.pallas import tpu as pltpu
from jax.sharding import PartitionSpec as P

STEPS = 4
RIM = 4
TS = 16
SUB = 32
NPATCH = 256
CAP = 3
EDGE = 16
WRITES = 4
COURANT = 0.6
LANES = 128
F32 = jnp.float32
BF16 = jnp.bfloat16


def iota(shape, dim):
    return lax.broadcasted_iota(jnp.int32, shape, dim)


def parts(x):
    high = x.astype(BF16)
    return high, (x - high.astype(F32)).astype(BF16)


def dot(a, b):
    return lax.dot_general(a, b, (((1,), (0,)), ((), ())), preferred_element_type=F32)


def dot_t(a, b):
    return lax.dot_general(a, b, (((1,), (1,)), ((), ())), preferred_element_type=F32)


def one_hot_dot(hot, x):
    high, low = parts(x)
    return dot(hot, high) + dot(hot, low)


def dot3(a, b, product=dot):
    a_high, a_low = parts(a)
    b_high, b_low = parts(b)
    return product(a_high, b_high) + (product(a_high, b_low) + product(a_low, b_high))


def spread_lon(basis_lon):
    tiles = LANES // TS
    tall = jnp.concatenate([basis_lon] * tiles, axis=0)
    inside = iota(tall.shape, 0) // SUB == iota(tall.shape, 1) // TS
    return jnp.where(inside, tall, 0.0)


def edge_columns(height, wet_depth):
    lane = iota(height.shape, 1)
    near = jnp.where(lane < EDGE, height, pltpu.roll(wet_depth, EDGE, 1))
    far = jnp.where(lane >= LANES - EDGE, height, pltpu.roll(wet_depth, LANES - EDGE, 1))
    return jnp.where(lane < LANES // 2, near, far)


def fetch(pairs, sems):
    copies = [pltpu.make_async_copy(src, dst, sems.at[i]) for i, (src, dst) in enumerate(pairs)]
    for copy in copies:
        copy.start()
    for copy in copies:
        copy.wait()


def prepare(h_ref, d_ref, w_ref, height_ref, wet_depth_ref, edge_ref, depth_buf, wet_buf, sems):
    fetch([(h_ref, height_ref), (d_ref, depth_buf), (w_ref, wet_buf)], sems)
    wet_depth = depth_buf[...] * wet_buf[...].astype(F32)
    wet_depth_ref[...] = wet_depth
    edge_ref[...] = edge_columns(height_ref[...], wet_depth).T


def tables(lat_ref, lon_ref, owner_ref, patch_ref, count_ref,
           lat4_ref, lon_high_ref, lon_low_ref, hot_ref, hot_t_ref, mask_ref):
    lat4_ref[...] = jnp.concatenate([lat_ref[...]] * 4, axis=0).T
    lon_high_ref[...], lon_low_ref[...] = parts(spread_lon(lon_ref[...]))

    def column(ref):
        table = ref[...].astype(F32).T
        flat = jnp.concatenate([table[:, k:k + 1] for k in range(table.shape[1])], axis=0)
        return jnp.broadcast_to(flat, (flat.shape[0], LANES))

    owner = column(owner_ref)
    patch = column(patch_ref)
    count = column(count_ref)
    owner_row = owner.T
    total = owner.shape[0]
    hot_t_ref[...] = (owner == iota(owner.shape, 1).astype(F32)).astype(BF16)
    hot_ref[...] = (owner_row == iota(owner_row.shape, 0).astype(F32)).astype(BF16)
    rank = jnp.zeros((total, LANES), F32)
    for q in range(total // LANES):
        row = jnp.broadcast_to(owner_row[0:1, q * LANES:(q + 1) * LANES], (total, LANES))
        earlier = iota((total, LANES), 1) + q * LANES < iota((total, LANES), 0)
        rank = rank + jnp.where(earlier & (row == owner), 1.0, 0.0)
    rank = jnp.broadcast_to(jnp.sum(rank, axis=1, keepdims=True), (total, LANES))
    lane = iota((total, LANES), 1)
    group = (lane // SUB).astype(F32)
    place = (lane % SUB).astype(F32)
    live = jnp.where((rank == group) & (place < count), 1.0, 0.0)
    number = jnp.where(rank == place, patch, 0.0)
    mask_ref[...] = jnp.where(lane < CAP * SUB, live, number)


def rims(parity_lat, ra, rb):
    south = jnp.where(parity_lat == 0, ra, rb)
    north = jnp.where(parity_lat == 0, rb, ra)
    return north, south


def corners(par_ref, edge_ref, ra_ref, rb_ref, first_ref, second_ref, strip_ref):
    north, south = rims(par_ref[1], ra_ref[...], rb_ref[...])
    block = jnp.concatenate(
        [
            edge_columns(south[0:8], south[8:16]),
            jnp.zeros((LANES - 16, LANES), F32),
            edge_columns(north[0:8], north[8:16]),
        ],
        axis=0,
    ).T
    rows = edge_ref.shape[1]
    strip_ref[0:2 * EDGE, 0:rows] = edge_ref[0:2 * EDGE, :]
    strip_ref[2 * EDGE:, 0:rows] = edge_ref[LANES - 2 * EDGE:, :]
    strip_ref[0:2 * EDGE, rows:] = block[0:2 * EDGE]
    strip_ref[2 * EDGE:, rows:] = block[LANES - 2 * EDGE:]
    west = jnp.concatenate([strip_ref[0:RIM, :], strip_ref[EDGE:EDGE + RIM, :]], axis=0)
    east = jnp.concatenate(
        [strip_ref[4 * EDGE - RIM:, :], strip_ref[3 * EDGE - RIM:3 * EDGE, :]], axis=0
    )
    first_ref[...] = jnp.where(par_ref[0] == 0, east, west)
    second_ref[...] = jnp.where(par_ref[0] == 0, west, east)


def march(height, wet_depth, right, below):
    def ahead(x, dim):
        return pltpu.roll(x, x.shape[dim] - 1, dim)

    ce = COURANT * jnp.minimum(wet_depth, ahead(wet_depth, right))
    cn = COURANT * jnp.minimum(wet_depth, ahead(wet_depth, below))
    east = jnp.zeros_like(height)
    north = jnp.zeros_like(height)
    for _ in range(STEPS):
        east = east + ce * (ahead(height, right) - height)
        north = north + cn * (ahead(height, below) - height)
        height = (
            height
            + COURANT * (east - pltpu.roll(east, 1, right))
            + COURANT * (north - pltpu.roll(north, 1, below))
        )
    return height


def inner(par_ref, height_ref, wet_depth_ref, ra_ref, rb_ref, out_ref):
    north, south = rims(par_ref[1], ra_ref[...], rb_ref[...])
    height = jnp.concatenate([north[0:8], height_ref[...], south[0:8]], axis=0)
    wet_depth = jnp.concatenate([north[8:16], wet_depth_ref[...], south[8:16]], axis=0)
    out_ref[...] = march(height, wet_depth, 1, 0)[8:8 + out_ref.shape[0]]


def forward(par_ref, inner_ref, strip_ref, ea_ref, eb_ref, lat4_ref, lon_high_ref, lon_low_ref,
            hot_ref, mask_ref, out_ref, send_ref, final_buf, sem):
    rows_own = inner_ref.shape[0]
    from_east = jnp.where(par_ref[0] == 0, ea_ref[...], eb_ref[...])
    from_west = jnp.where(par_ref[0] == 0, eb_ref[...], ea_ref[...])
    keep = EDGE - RIM
    west = march(
        jnp.concatenate([from_west[0:RIM], strip_ref[0:keep, :]], axis=0),
        jnp.concatenate([from_west[RIM:], strip_ref[EDGE:EDGE + keep, :]], axis=0),
        0, 1,
    )
    east = march(
        jnp.concatenate([strip_ref[3 * EDGE + RIM:, :], from_east[0:RIM]], axis=0),
        jnp.concatenate([strip_ref[2 * EDGE + RIM:3 * EDGE, :], from_east[RIM:]], axis=0),
        0, 1,
    )
    lanes = west.shape[1]
    table = jnp.concatenate(
        [west[RIM:2 * RIM], jnp.zeros((LANES - 2 * RIM, lanes), F32), east[EDGE - 2 * RIM:EDGE - RIM]],
        axis=0,
    )[:, :rows_own].T
    lane = iota((rows_own, LANES), 1)
    final = jnp.where((lane < RIM) | (lane >= LANES - RIM), table, inner_ref[...])
    final_buf[...] = final
    write = pltpu.make_async_copy(final_buf, out_ref, sem)
    write.start()

    high, low = parts(final)
    product = dot_t(high, lon_high_ref[...]) + (
        dot_t(high, lon_low_ref[...]) + dot_t(low, lon_high_ref[...])
    )
    lat4 = lat4_ref[...]
    product = product * jnp.concatenate([lat4, lat4], axis=1)
    tile_rows = rows_own // TS
    sums = jnp.sum(product.reshape(tile_rows, TS, product.shape[1]), axis=1)
    group = iota((tile_rows, LANES), 1) // SUB
    stacked = []
    for q in range(sums.shape[1] // LANES):
        for g in range(4):
            own = jnp.where(group == g, sums[:, q * LANES:(q + 1) * LANES], 0.0)
            own = own + pltpu.roll(own, 2 * SUB, 1)
            stacked.append(own + pltpu.roll(own, SUB, 1))
    values = jnp.concatenate(stacked, axis=0)
    mask = mask_ref[...]
    filled = jnp.where(iota(mask.shape, 1) < CAP * SUB, values * mask, mask)
    send_ref[...] = one_hot_dot(hot_ref[...], filled)
    write.wait()


def smooth(recv_ref, prior_ref, sub_ref, reply_ref):
    received = recv_ref[...]
    turned = received.T
    devices = received.shape[0]
    group = iota((devices, LANES), 1) // SUB
    gathered = jnp.zeros((NPATCH, LANES), F32)
    for r in range(CAP):
        line = jnp.broadcast_to(turned[CAP * SUB + r:CAP * SUB + r + 1], (NPATCH, devices))
        member = (line == iota((NPATCH, devices), 0).astype(F32)).astype(BF16)
        gathered = gathered + one_hot_dot(member, jnp.where(group == r, received, 0.0))
    mixed = dot3(prior_ref[...], gathered)
    sub = jnp.concatenate([sub_ref[...]] * 4, axis=1)
    sub = jnp.concatenate([sub] * CAP + [jnp.zeros_like(sub)], axis=0)
    smoothed = dot3(mixed, sub)
    group = iota(smoothed.shape, 1) // SUB
    reply = jnp.zeros((devices, LANES), F32)
    for r in range(CAP):
        line = jnp.broadcast_to(received[:, CAP * SUB + r:CAP * SUB + r + 1], (devices, NPATCH))
        member = (line == iota((devices, NPATCH), 1).astype(F32)).astype(BF16)
        reply = reply + one_hot_dot(member, jnp.where(group == r, smoothed, 0.0))
    reply_ref[...] = reply


def backward(ret_ref, hot_t_ref, mask_ref, lat4_ref, lon_high_ref, lon_low_ref, out_ref, buf, sems):
    mask = mask_ref[...]
    picked = one_hot_dot(hot_t_ref[...], ret_ref[...])
    picked = jnp.where(iota(mask.shape, 1) < CAP * SUB, picked * mask, 0.0)
    picked = picked + pltpu.roll(picked, 2 * SUB, 1)
    picked = picked + pltpu.roll(picked, SUB, 1)
    rows = buf.shape[0]
    tile_rows = rows // TS
    group = iota((tile_rows, LANES), 1) // SUB
    halves = []
    for q in range(2):
        half = picked[4 * q * tile_rows:(4 * q + 1) * tile_rows]
        for g in range(1, 4):
            block = picked[(4 * q + g) * tile_rows:(4 * q + g + 1) * tile_rows]
            half = jnp.where(group == g, block, half)
        halves.append(half)
    value = jnp.concatenate(halves, axis=1)
    lon_high, lon_low = lon_high_ref[...], lon_low_ref[...]
    writes = []
    share = rows // WRITES
    for i in range(WRITES):
        part = value[i * share // TS:(i + 1) * share // TS]
        wide = jnp.broadcast_to(part[:, None, :], (share // TS, TS, part.shape[1]))
        lat4 = lat4_ref[i * share:(i + 1) * share, :]
        high, low = parts(wide.reshape(share, part.shape[1]) * jnp.concatenate([lat4, lat4], axis=1))
        buf[i * share:(i + 1) * share, :] = dot(high, lon_high) + (dot(high, lon_low) + dot(low, lon_high))
        span = pl.ds(i * share, share)
        writes.append(pltpu.make_async_copy(buf.at[span], out_ref.at[span], sems.at[i]))
        writes[-1].start()
    for write in writes:
        write.wait()


VMEM = pl.BlockSpec(memory_space=pltpu.VMEM)
SMEM = pl.BlockSpec(memory_space=pltpu.SMEM)
HBM = pl.BlockSpec(memory_space=pltpu.HBM)


def call(kernel, ins, outs, *args, scratch=()):
    return pl.pallas_call(
        kernel,
        out_shape=[jax.ShapeDtypeStruct(shape, dtype) for shape, dtype, _ in outs],
        in_specs=ins,
        out_specs=[spec for _, _, spec in outs],
        scratch_shapes=scratch,
        compiler_params=pltpu.CompilerParams(vmem_limit_bytes=32 * 1024 * 1024),
    )(*args)


def swap_pairs(axis, first, periodic):
    count = lax.axis_size(axis)
    pairs = []
    for a in range(first, count, 2):
        b = a + 1
        if b == count:
            if not periodic:
                continue
            b = 0
        pairs += [(a, b), (b, a)]
    return pairs


def swap(payload, axis, periodic):
    if axis == "lat":
        second = lax.ppermute(payload[1], axis, swap_pairs(axis, 1, periodic))
        late, _ = lax.optimization_barrier((payload[0], payload[1]))
        return lax.ppermute(late, axis, swap_pairs(axis, 0, periodic)), second
    late, _ = lax.optimization_barrier((payload[1], payload[0]))
    second = lax.ppermute(late, axis, swap_pairs(axis, 1, periodic))
    return lax.ppermute(payload[0], axis, swap_pairs(axis, 0, periodic)), second


def local(
    adjoint_height,
    depth,
    wet,
    basis_lat,
    basis_lon,
    tile_owner,
    tile_patch,
    tile_count,
    prior_patches,
    prior_subfaults,
):
    rows, cols = adjoint_height.shape
    lon_devices = lax.axis_size("lon")
    total = (rows // TS) * (cols // TS)
    parity = jnp.stack([lax.axis_index("lon") & 1, lax.axis_index("lat") & 1]).astype(jnp.int32)

    def edge_rows(start):
        def cut(x):
            return lax.dynamic_slice_in_dim(x, start, 8, axis=0)
        return jnp.concatenate([cut(adjoint_height), cut(depth) * cut(wet).astype(F32)], axis=0)

    last = (rows - 8) * (1 - parity[1])
    north_a, north_b = swap([edge_rows(last), edge_rows(rows - 8 - last)], "lat", False)
    dma = pltpu.SemaphoreType.DMA
    own = pltpu.VMEM((rows, cols), F32)
    height, wet_depth, edges = call(
        prepare,
        [HBM] * 3,
        [((rows, cols), F32, VMEM), ((rows, cols), F32, VMEM), ((LANES, rows), F32, VMEM)],
        *[pltpu.with_memory_space_constraint(x, pltpu.HBM) for x in (adjoint_height, depth, wet)],
        scratch=[own, pltpu.VMEM((rows, cols), jnp.int32), dma((3,))],
    )
    lat4, lon_high, lon_low, hot, hot_t, mask = call(
        tables,
        [VMEM] * 5,
        [
            ((rows, LANES), F32, VMEM),
            ((total, LANES), BF16, VMEM),
            ((total, LANES), BF16, VMEM),
            ((lon_devices, total), BF16, VMEM),
            ((total, lon_devices), BF16, VMEM),
            ((total, LANES), F32, VMEM),
        ],
        basis_lat, basis_lon, tile_owner.T, tile_patch.T, tile_count.T,
    )
    first, second, strips = call(
        corners,
        [SMEM] + [VMEM] * 3,
        [((2 * RIM, rows + LANES), F32, VMEM)] * 2 + [((4 * EDGE, rows + LANES), F32, VMEM)],
        parity, edges, north_a, north_b,
    )
    east_a, east_b = swap([first, second], "lon", True)
    (middle,) = call(
        inner, [SMEM] + [VMEM] * 4, [((rows, cols), F32, VMEM)],
        parity, height, wet_depth, north_a, north_b,
    )
    final, sent = call(
        forward,
        [SMEM] + [VMEM] * 9,
        [((rows, cols), F32, HBM), ((lon_devices, LANES), F32, VMEM)],
        parity, middle, strips, east_a, east_b, lat4, lon_high, lon_low, hot, mask,
        scratch=[own, dma(())],
    )
    received = lax.all_to_all(sent, "lon", split_axis=0, concat_axis=0, tiled=True)
    (replies,) = call(
        smooth,
        [VMEM] * 3,
        [((lon_devices, LANES), F32, VMEM)],
        received, prior_patches.reshape(NPATCH, NPATCH), prior_subfaults,
    )
    returned = lax.all_to_all(replies, "lon", split_axis=0, concat_axis=0, tiled=True)
    (gradient,) = call(
        backward,
        [VMEM] * 6,
        [((rows, cols), F32, HBM)],
        returned, hot_t, mask, lat4, lon_high, lon_low,
        scratch=[own, dma((WRITES,))],
    )
    return (final, gradient)


def solution(mesh):
    return jax.shard_map(
        local,
        mesh=mesh,
        in_specs=(
            P("lat", "lon"),
            P("lat", "lon"),
            P("lat", "lon"),
            P(None, "lat"),
            P(None, "lon"),
            P("lat", "lon"),
            P("lat", "lon"),
            P("lat", "lon"),
            P("lat", "lon", None, None),
            P(),
        ),
        out_specs=(P("lat", "lon"), P("lat", "lon")),
        check_vma=False,
    )
```

```python
import jax
import jax.numpy as jnp
from jax import lax
from jax.experimental import pallas as pl
from jax.experimental.pallas import tpu as pltpu
from jax.sharding import PartitionSpec as P

STEPS = 4
RIM = 4
TS = 16
SUB = 32
NPATCH = 256
CAP = 3
EDGE = 8
WRITES = 4
COURANT = 0.6
LANES = 128
F32 = jnp.float32
BF16 = jnp.bfloat16


def iota(shape, dim):
    return lax.broadcasted_iota(jnp.int32, shape, dim)


def parts(x):
    high = x.astype(BF16)
    return high, (x - high.astype(F32)).astype(BF16)


def dot(a, b):
    return lax.dot_general(a, b, (((1,), (0,)), ((), ())), preferred_element_type=F32)


def join_cols(*blocks):
    return jnp.concatenate(blocks, axis=1)


def join_rows(*blocks):
    return jnp.concatenate(blocks, axis=0)


def fold(x):
    return x[:, :LANES] + x[:, LANES:]


def spread_lon(basis_lon):
    tiles = LANES // TS
    tall = join_rows(*[basis_lon] * tiles)
    inside = iota(tall.shape, 0) // SUB == iota(tall.shape, 1) // TS
    return jnp.where(inside, tall, 0.0)


def edge_columns(height, wet_depth):
    lane = iota(height.shape, 1)
    near = jnp.where(lane < EDGE, height, pltpu.roll(wet_depth, EDGE, 1))
    far = jnp.where(lane >= LANES - EDGE, height, pltpu.roll(wet_depth, LANES - EDGE, 1))
    return jnp.where(lane < LANES // 2, near, far)


def pick_edges(turned):
    return join_rows(turned[0:2 * EDGE], turned[LANES - 2 * EDGE:])


def prepare(lat_hbm, lon_hbm, owner_hbm, patch_hbm, count_hbm, h_hbm, d_hbm, w_hbm,
            height_ref, wet_depth_ref, edge_ref, lat4_ref, lon_ref, lon_t_ref, hot_ref, hot_t_ref,
            mask_ref, lat_buf, lon_buf, owner_buf, patch_buf, count_buf, depth_buf, wet_buf, sems):
    pairs = [(lat_hbm, lat_buf), (lon_hbm, lon_buf), (owner_hbm, owner_buf), (patch_hbm, patch_buf),
             (count_hbm, count_buf), (h_hbm, height_ref), (d_hbm, depth_buf), (w_hbm, wet_buf)]
    copies = [pltpu.make_async_copy(src, dst, sems.at[i]) for i, (src, dst) in enumerate(pairs)]
    for copy in copies:
        copy.start()
    for copy in copies[:5]:
        copy.wait()
    lat4_ref[...] = join_rows(*[lat_buf[...]] * 4).T
    spread = spread_lon(lon_buf[...])
    lon_ref[...] = join_cols(*parts(spread))
    lon_t_ref[...] = join_rows(*parts(spread.T))

    def column(ref):
        table = ref[...].astype(F32).T
        flat = join_rows(*[table[:, k:k + 1] for k in range(table.shape[1])])
        return jnp.broadcast_to(flat, (flat.shape[0], LANES))

    owner = column(owner_buf)
    patch = column(patch_buf)
    count = column(count_buf)
    owner_row = owner.T
    total = owner.shape[0]
    hot_t = (owner == iota(owner.shape, 1).astype(F32)).astype(BF16)
    hot_t_ref[...] = join_cols(hot_t, hot_t)
    hot_ref[...] = (owner_row == iota(owner_row.shape, 0).astype(F32)).astype(BF16)
    rank = jnp.zeros((total, LANES), F32)
    for q in range(total // LANES):
        row = jnp.broadcast_to(owner_row[0:1, q * LANES:(q + 1) * LANES], (total, LANES))
        earlier = iota((total, LANES), 1) + q * LANES < iota((total, LANES), 0)
        rank = rank + jnp.where(earlier & (row == owner), 1.0, 0.0)
    rank = jnp.broadcast_to(jnp.sum(rank, axis=1, keepdims=True), (total, LANES))
    lane = iota((total, LANES), 1)
    group = (lane // SUB).astype(F32)
    place = (lane % SUB).astype(F32)
    live = jnp.where((rank == group) & (place < count), 1.0, 0.0)
    number = jnp.where(rank == place, patch, 0.0)
    mask_ref[...] = jnp.where(lane < CAP * SUB, live, number)

    for copy in copies[5:]:
        copy.wait()
    wet_depth = depth_buf[...] * wet_buf[...].astype(F32)
    wet_depth_ref[...] = wet_depth
    edge_ref[...] = pick_edges(edge_columns(height_ref[...], wet_depth).T)


def rims(parity_lat, ra, rb):
    south = jnp.where(parity_lat == 0, ra, rb)
    north = jnp.where(parity_lat == 0, rb, ra)
    return north, south


def corners(par_ref, edge_ref, ra_ref, rb_ref, first_ref, second_ref, block_ref):
    north, south = rims(par_ref[1], ra_ref[...], rb_ref[...])
    block = join_rows(
        edge_columns(south[0:8], south[8:16]),
        jnp.zeros((LANES - 16, LANES), F32),
        edge_columns(north[0:8], north[8:16]),
    ).T
    block = pick_edges(block)
    block_ref[...] = block
    strips = join_cols(edge_ref[...], block)
    west = join_rows(strips[0:RIM], strips[EDGE:EDGE + RIM])
    east = join_rows(strips[4 * EDGE - RIM:], strips[3 * EDGE - RIM:3 * EDGE])
    first_ref[...] = jnp.where(par_ref[0] == 0, east, west)
    second_ref[...] = jnp.where(par_ref[0] == 0, west, east)


def march(height, wet_depth, right, below):
    def ahead(x, dim):
        return pltpu.roll(x, x.shape[dim] - 1, dim)

    ce = COURANT * jnp.minimum(wet_depth, ahead(wet_depth, right))
    cn = COURANT * jnp.minimum(wet_depth, ahead(wet_depth, below))
    east = jnp.zeros_like(height)
    north = jnp.zeros_like(height)
    for _ in range(STEPS):
        east = east + ce * (ahead(height, right) - height)
        north = north + cn * (ahead(height, below) - height)
        height = (
            height
            + COURANT * (east - pltpu.roll(east, 1, right))
            + COURANT * (north - pltpu.roll(north, 1, below))
        )
    return height


def inner(par_ref, height_ref, wet_depth_ref, ra_ref, rb_ref, out_ref):
    north, south = rims(par_ref[1], ra_ref[...], rb_ref[...])
    height = join_rows(north[0:8], height_ref[...], south[0:8])
    wet_depth = join_rows(north[8:16], wet_depth_ref[...], south[8:16])
    out_ref[...] = march(height, wet_depth, 1, 0)[8:8 + out_ref.shape[0]]


def forward(par_ref, inner_ref, edge_ref, block_ref, ea_ref, eb_ref, lat4_ref, lon_t_ref,
            hot_ref, mask_ref, out_ref, send_ref, final_buf, sem):
    rows_own = inner_ref.shape[0]
    from_east = jnp.where(par_ref[0] == 0, ea_ref[...], eb_ref[...])
    from_west = jnp.where(par_ref[0] == 0, eb_ref[...], ea_ref[...])
    own = join_cols(edge_ref[...], block_ref[...])
    strip = march(
        join_rows(from_west[0:RIM], own[0:EDGE], own[3 * EDGE:], from_east[0:RIM]),
        join_rows(from_west[RIM:], own[EDGE:2 * EDGE], own[2 * EDGE:3 * EDGE], from_east[RIM:]),
        0, 1,
    )[:, :rows_own]
    table = join_rows(
        strip[RIM:2 * RIM], jnp.zeros((LANES - 2 * RIM, rows_own), F32), strip[2 * EDGE:2 * EDGE + RIM]
    ).T
    lane = iota((rows_own, LANES), 1)
    final = jnp.where((lane < RIM) | (lane >= LANES - RIM), table, inner_ref[...])
    final_buf[...] = final
    write = pltpu.make_async_copy(final_buf, out_ref, sem)
    write.start()

    high, low = parts(final)
    lon_high, lon_low = lon_t_ref[:LANES, :], lon_t_ref[LANES:, :]
    product = dot(join_cols(high, low), join_rows(lon_high, lon_high)) + dot(high, lon_low)
    lat4 = lat4_ref[...]
    product = product * join_cols(lat4, lat4)
    tile_rows = rows_own // TS
    sums = jnp.sum(product.reshape(tile_rows, TS, product.shape[1]), axis=1)
    group = iota((tile_rows, LANES), 1) // SUB
    stacked = []
    for q in range(sums.shape[1] // LANES):
        for g in range(4):
            part = jnp.where(group == g, sums[:, q * LANES:(q + 1) * LANES], 0.0)
            part = part + pltpu.roll(part, 2 * SUB, 1)
            stacked.append(part + pltpu.roll(part, SUB, 1))
    values = join_rows(*stacked)
    mask = mask_ref[...]
    filled = jnp.where(iota(mask.shape, 1) < CAP * SUB, values * mask, mask)
    send_ref[...] = fold(dot(hot_ref[...], join_cols(*parts(filled))))
    write.wait()


def smooth(recv_ref, prior_ref, sub_ref, reply_ref):
    received = recv_ref[...]
    turned = received.T
    devices = received.shape[0]
    group = iota((devices, 2 * LANES), 1) % LANES // SUB
    both = join_cols(*parts(received))

    def members(r):
        line = jnp.broadcast_to(turned[CAP * SUB + r:CAP * SUB + r + 1], (NPATCH, devices))
        return (line == iota((NPATCH, devices), 0).astype(F32)).astype(BF16)

    def share(r):
        return jnp.where(group == r, both, jnp.zeros_like(both))

    gathered = fold(
        dot(join_cols(members(0), members(1)), join_rows(share(0), share(1))) + dot(members(2), share(2))
    )
    prior_high, prior_low = parts(prior_ref[...])
    high, low = parts(gathered)
    mixed = fold(dot(prior_high, join_cols(high, low))) + dot(prior_low, high)
    sub = join_cols(*[sub_ref[...]] * 4)
    sub_high, sub_low = parts(join_rows(*[sub] * CAP, jnp.zeros_like(sub)))
    high, low = parts(mixed)
    smoothed = dot(join_cols(high, low), join_rows(sub_high, sub_high)) + dot(high, sub_low)
    both = join_cols(*parts(smoothed))
    group = iota((devices, LANES), 1) // SUB
    reply = None
    for r in range(CAP):
        line = jnp.broadcast_to(received[:, CAP * SUB + r:CAP * SUB + r + 1], (devices, NPATCH))
        member = (line == iota((devices, NPATCH), 1).astype(F32)).astype(BF16)
        found = fold(dot(member, both))
        reply = found if reply is None else jnp.where(group == r, found, reply)
    reply_ref[...] = reply


def backward(ret_ref, hot_t_ref, mask_ref, lat4_ref, lon_ref, out_ref, buf, sems):
    mask = mask_ref[...]
    picked = dot(hot_t_ref[...], join_rows(*parts(ret_ref[...])))
    picked = jnp.where(iota(mask.shape, 1) < CAP * SUB, picked * mask, 0.0)
    picked = picked + pltpu.roll(picked, 2 * SUB, 1)
    picked = picked + pltpu.roll(picked, SUB, 1)
    rows = buf.shape[0]
    tile_rows = rows // TS
    group = iota((tile_rows, LANES), 1) // SUB
    halves = []
    for q in range(2):
        half = picked[4 * q * tile_rows:(4 * q + 1) * tile_rows]
        for g in range(1, 4):
            block = picked[(4 * q + g) * tile_rows:(4 * q + g + 1) * tile_rows]
            half = jnp.where(group == g, block, half)
        halves.append(half)
    value = join_cols(*halves)
    lon = lon_ref[...]
    writes = []
    share = rows // WRITES
    for i in range(WRITES):
        part = value[i * share // TS:(i + 1) * share // TS]
        wide = jnp.broadcast_to(part[:, None, :], (share // TS, TS, part.shape[1]))
        lat4 = lat4_ref[i * share:(i + 1) * share, :]
        high, low = parts(wide.reshape(share, part.shape[1]) * join_cols(lat4, lat4))
        buf[i * share:(i + 1) * share, :] = fold(dot(high, lon)) + dot(low, lon[:, :LANES])
        span = pl.ds(i * share, share)
        writes.append(pltpu.make_async_copy(buf.at[span], out_ref.at[span], sems.at[i]))
        writes[-1].start()
    for write in writes:
        write.wait()


VMEM = pl.BlockSpec(memory_space=pltpu.VMEM)
SMEM = pl.BlockSpec(memory_space=pltpu.SMEM)
HBM = pl.BlockSpec(memory_space=pltpu.HBM)


def call(kernel, ins, outs, *args, scratch=()):
    return pl.pallas_call(
        kernel,
        out_shape=[jax.ShapeDtypeStruct(shape, dtype) for shape, dtype, _ in outs],
        in_specs=ins,
        out_specs=[spec for _, _, spec in outs],
        scratch_shapes=scratch,
        compiler_params=pltpu.CompilerParams(vmem_limit_bytes=32 * 1024 * 1024),
    )(*args)


def swap_pairs(axis, first, periodic):
    count = lax.axis_size(axis)
    pairs = []
    for a in range(first, count, 2):
        b = a + 1
        if b == count:
            if not periodic:
                continue
            b = 0
        pairs += [(a, b), (b, a)]
    return pairs


def swap(payload, axis, periodic):
    if axis == "lat":
        second = lax.ppermute(payload[1], axis, swap_pairs(axis, 1, periodic))
        late, _ = lax.optimization_barrier((payload[0], payload[1]))
        return lax.ppermute(late, axis, swap_pairs(axis, 0, periodic)), second
    late, _ = lax.optimization_barrier((payload[1], payload[0]))
    second = lax.ppermute(late, axis, swap_pairs(axis, 1, periodic))
    return lax.ppermute(payload[0], axis, swap_pairs(axis, 0, periodic)), second


def local(
    adjoint_height,
    depth,
    wet,
    basis_lat,
    basis_lon,
    tile_owner,
    tile_patch,
    tile_count,
    prior_patches,
    prior_subfaults,
):
    rows, cols = adjoint_height.shape
    lon_devices = lax.axis_size("lon")
    total = (rows // TS) * (cols // TS)
    parity = jnp.stack([lax.axis_index("lon") & 1, lax.axis_index("lat") & 1]).astype(jnp.int32)

    def edge_rows(start):
        def cut(x):
            return lax.dynamic_slice_in_dim(x, start, 8, axis=0)
        return jnp.concatenate([cut(adjoint_height), cut(depth) * cut(wet).astype(F32)], axis=0)

    last = (rows - 8) * (1 - parity[1])
    north_a, north_b = swap([edge_rows(last), edge_rows(rows - 8 - last)], "lat", False)
    dma = pltpu.SemaphoreType.DMA
    own = pltpu.VMEM((rows, cols), F32)
    tile_shape = (cols // TS, rows // TS)
    resident = [
        basis_lat, basis_lon, tile_owner.T, tile_patch.T, tile_count.T, adjoint_height, depth, wet
    ]
    height, wet_depth, edges, lat4, lon, lon_t, hot, hot_t, mask = call(
        prepare,
        [HBM] * len(resident),
        [
            ((rows, cols), F32, VMEM),
            ((rows, cols), F32, VMEM),
            ((4 * EDGE, rows), F32, VMEM),
            ((rows, LANES), F32, VMEM),
            ((total, 2 * LANES), BF16, VMEM),
            ((2 * LANES, total), BF16, VMEM),
            ((lon_devices, total), BF16, VMEM),
            ((total, 2 * lon_devices), BF16, VMEM),
            ((total, LANES), F32, VMEM),
        ],
        *[pltpu.with_memory_space_constraint(x, pltpu.HBM) for x in resident],
        scratch=[pltpu.VMEM((SUB, rows), F32), pltpu.VMEM((SUB, cols), F32)]
        + [pltpu.VMEM(tile_shape, jnp.int32)] * 3
        + [own, pltpu.VMEM((rows, cols), jnp.int32), dma((len(resident),))],
    )
    payload = ((2 * RIM, rows + LANES), F32, VMEM)
    first, second, block = call(
        corners,
        [SMEM] + [VMEM] * 3,
        [payload, payload, ((4 * EDGE, LANES), F32, VMEM)],
        parity, edges, north_a, north_b,
    )
    east_a, east_b = swap([first, second], "lon", True)
    (middle,) = call(
        inner, [SMEM] + [VMEM] * 4, [((rows, cols), F32, VMEM)],
        parity, height, wet_depth, north_a, north_b,
    )
    final, sent = call(
        forward,
        [SMEM] + [VMEM] * 9,
        [((rows, cols), F32, HBM), ((lon_devices, LANES), F32, VMEM)],
        parity, middle, edges, block, east_a, east_b, lat4, lon_t, hot, mask,
        scratch=[own, dma(())],
    )
    received = lax.all_to_all(sent, "lon", split_axis=0, concat_axis=0, tiled=True)
    (replies,) = call(
        smooth,
        [VMEM] * 3,
        [((lon_devices, LANES), F32, VMEM)],
        received, prior_patches.reshape(NPATCH, NPATCH), prior_subfaults,
    )
    returned = lax.all_to_all(replies, "lon", split_axis=0, concat_axis=0, tiled=True)
    (gradient,) = call(
        backward,
        [VMEM] * 5,
        [((rows, cols), F32, HBM)],
        returned, hot_t, mask, lat4, lon,
        scratch=[own, dma((WRITES,))],
    )
    return (final, gradient)


def solution(mesh):
    return jax.shard_map(
        local,
        mesh=mesh,
        in_specs=(
            P("lat", "lon"),
            P("lat", "lon"),
            P("lat", "lon"),
            P(None, "lat"),
            P(None, "lon"),
            P("lat", "lon"),
            P("lat", "lon"),
            P("lat", "lon"),
            P("lat", "lon", None, None),
            P(),
        ),
        out_specs=(P("lat", "lon"), P("lat", "lon")),
        check_vma=False,
    )
```

```python
import jax
import jax.numpy as jnp
from jax import lax
from jax.experimental import pallas as pl
from jax.experimental.pallas import tpu as pltpu
from jax.sharding import PartitionSpec as P

STEPS = 4
RIM = 4
TS = 16
SUB = 32
NPATCH = 256
CAP = 3
EDGE = 8
WRITES = 4
COURANT = 0.6
LANES = 128
F32 = jnp.float32
BF16 = jnp.bfloat16


def iota(shape, dim):
    return lax.broadcasted_iota(jnp.int32, shape, dim)


def parts(x):
    high = x.astype(BF16)
    return high, (x - high.astype(F32)).astype(BF16)


def dot(a, b):
    return lax.dot_general(a, b, (((1,), (0,)), ((), ())), preferred_element_type=F32)


def join_cols(*blocks):
    return jnp.concatenate(blocks, axis=1)


def join_rows(*blocks):
    return jnp.concatenate(blocks, axis=0)


def fold(x):
    return x[:, :LANES] + x[:, LANES:]


def spread_lon(basis_lon):
    tiles = LANES // TS
    tall = join_rows(*[basis_lon] * tiles)
    inside = iota(tall.shape, 0) // SUB == iota(tall.shape, 1) // TS
    return jnp.where(inside, tall, 0.0)


def edge_columns(height, wet_depth):
    lane = iota(height.shape, 1)
    near = jnp.where(lane < EDGE, height, pltpu.roll(wet_depth, EDGE, 1))
    far = jnp.where(lane >= LANES - EDGE, height, pltpu.roll(wet_depth, LANES - EDGE, 1))
    return jnp.where(lane < LANES // 2, near, far)


def pick_edges(turned):
    return join_rows(turned[0:2 * EDGE], turned[LANES - 2 * EDGE:])


def prepare(lat_hbm, lon_hbm, owner_hbm, patch_hbm, count_hbm, h_hbm, d_hbm, w_hbm,
            height_ref, wet_depth_ref, edge_ref, lat4_ref, lon_ref, lon_t_ref, hot_ref, hot_t_ref,
            mask_ref, lat_buf, lon_buf, owner_buf, patch_buf, count_buf, depth_buf, wet_buf, sems):
    pairs = [(lat_hbm, lat_buf), (lon_hbm, lon_buf), (owner_hbm, owner_buf), (patch_hbm, patch_buf),
             (count_hbm, count_buf), (h_hbm, height_ref), (d_hbm, depth_buf), (w_hbm, wet_buf)]
    copies = [pltpu.make_async_copy(src, dst, sems.at[i]) for i, (src, dst) in enumerate(pairs)]
    for copy in copies:
        copy.start()
    for copy in copies[:5]:
        copy.wait()
    lat4_ref[...] = join_rows(*[lat_buf[...]] * 4).T
    spread = spread_lon(lon_buf[...])
    lon_ref[...] = join_cols(*parts(spread))
    lon_t_ref[...] = join_rows(*parts(spread.T))

    def column(ref):
        table = ref[...].astype(F32).T
        flat = join_rows(*[table[:, k:k + 1] for k in range(table.shape[1])])
        return jnp.broadcast_to(flat, (flat.shape[0], LANES))

    owner = column(owner_buf)
    patch = column(patch_buf)
    count = column(count_buf)
    owner_row = owner.T
    total = owner.shape[0]
    hot_t = (owner == iota(owner.shape, 1).astype(F32)).astype(BF16)
    hot_t_ref[...] = join_cols(hot_t, hot_t)
    hot_ref[...] = (owner_row == iota(owner_row.shape, 0).astype(F32)).astype(BF16)
    rank = jnp.zeros((total, LANES), F32)
    for q in range(total // LANES):
        row = jnp.broadcast_to(owner_row[0:1, q * LANES:(q + 1) * LANES], (total, LANES))
        earlier = iota((total, LANES), 1) + q * LANES < iota((total, LANES), 0)
        rank = rank + jnp.where(earlier & (row == owner), 1.0, 0.0)
    rank = jnp.broadcast_to(jnp.sum(rank, axis=1, keepdims=True), (total, LANES))
    lane = iota((total, LANES), 1)
    group = (lane // SUB).astype(F32)
    place = (lane % SUB).astype(F32)
    live = jnp.where((rank == group) & (place < count), 1.0, 0.0)
    number = jnp.where(rank == place, patch, 0.0)
    mask_ref[...] = jnp.where(lane < CAP * SUB, live, number)

    for copy in copies[5:]:
        copy.wait()
    wet_depth = depth_buf[...] * wet_buf[...].astype(F32)
    wet_depth_ref[...] = wet_depth
    edge_ref[...] = pick_edges(edge_columns(height_ref[...], wet_depth).T)


def is_even(axis):
    return (lax.axis_index(axis) & 1) == 0


def rims(ra, rb):
    even = is_even("lat")
    return jnp.where(even, rb, ra), jnp.where(even, ra, rb)


def corners(edge_ref, ra_ref, rb_ref, first_ref, second_ref, block_ref):
    north, south = rims(ra_ref[...], rb_ref[...])
    block = join_rows(
        edge_columns(south[0:8], south[8:16]),
        jnp.zeros((LANES - 16, LANES), F32),
        edge_columns(north[0:8], north[8:16]),
    ).T
    block = pick_edges(block)
    block_ref[...] = block
    strips = join_cols(edge_ref[...], block)
    west = join_rows(strips[0:RIM], strips[EDGE:EDGE + RIM])
    east = join_rows(strips[4 * EDGE - RIM:], strips[3 * EDGE - RIM:3 * EDGE])
    even = is_even("lon")
    first_ref[...] = jnp.where(even, east, west)
    second_ref[...] = jnp.where(even, west, east)


def march(height, wet_depth, right, below):
    def ahead(x, dim):
        return pltpu.roll(x, x.shape[dim] - 1, dim)

    ce = COURANT * jnp.minimum(wet_depth, ahead(wet_depth, right))
    cn = COURANT * jnp.minimum(wet_depth, ahead(wet_depth, below))
    east = jnp.zeros_like(height)
    north = jnp.zeros_like(height)
    for _ in range(STEPS):
        east = east + ce * (ahead(height, right) - height)
        north = north + cn * (ahead(height, below) - height)
        height = (
            height
            + COURANT * (east - pltpu.roll(east, 1, right))
            + COURANT * (north - pltpu.roll(north, 1, below))
        )
    return height


def inner(height_ref, wet_depth_ref, ra_ref, rb_ref, out_ref):
    north, south = rims(ra_ref[...], rb_ref[...])
    height = join_rows(north[0:8], height_ref[...], south[0:8])
    wet_depth = join_rows(north[8:16], wet_depth_ref[...], south[8:16])
    out_ref[...] = march(height, wet_depth, 1, 0)[8:8 + out_ref.shape[0]]


def forward(inner_ref, edge_ref, block_ref, ea_ref, eb_ref, lat4_ref, lon_t_ref,
            hot_ref, mask_ref, final_ref, send_ref):
    rows_own = inner_ref.shape[0]
    even = is_even("lon")
    from_east = jnp.where(even, ea_ref[...], eb_ref[...])
    from_west = jnp.where(even, eb_ref[...], ea_ref[...])
    own = join_cols(edge_ref[...], block_ref[...])
    strip = march(
        join_rows(from_west[0:RIM], own[0:EDGE], own[3 * EDGE:], from_east[0:RIM]),
        join_rows(from_west[RIM:], own[EDGE:2 * EDGE], own[2 * EDGE:3 * EDGE], from_east[RIM:]),
        0, 1,
    )[:, :rows_own]
    table = join_rows(
        strip[RIM:2 * RIM], jnp.zeros((LANES - 2 * RIM, rows_own), F32), strip[2 * EDGE:2 * EDGE + RIM]
    ).T
    lane = iota((rows_own, LANES), 1)
    final = jnp.where((lane < RIM) | (lane >= LANES - RIM), table, inner_ref[...])
    final_ref[...] = final

    high, low = parts(final)
    lon_high, lon_low = lon_t_ref[:LANES, :], lon_t_ref[LANES:, :]
    product = dot(join_cols(high, low), join_rows(lon_high, lon_high)) + dot(high, lon_low)
    lat4 = lat4_ref[...]
    product = product * join_cols(lat4, lat4)
    tile_rows = rows_own // TS
    sums = jnp.sum(product.reshape(tile_rows, TS, product.shape[1]), axis=1)
    group = iota((tile_rows, LANES), 1) // SUB
    stacked = []
    for q in range(sums.shape[1] // LANES):
        for g in range(4):
            part = jnp.where(group == g, sums[:, q * LANES:(q + 1) * LANES], 0.0)
            part = part + pltpu.roll(part, 2 * SUB, 1)
            stacked.append(part + pltpu.roll(part, SUB, 1))
    values = join_rows(*stacked)
    mask = mask_ref[...]
    filled = jnp.where(iota(mask.shape, 1) < CAP * SUB, values * mask, mask)
    send_ref[...] = fold(dot(hot_ref[...], join_cols(*parts(filled))))


def smooth(recv_ref, prior_ref, sub_ref, final_ref, reply_ref, out_ref, sem):
    write = pltpu.make_async_copy(final_ref, out_ref, sem)
    write.start()
    received = recv_ref[...]
    turned = received.T
    devices = received.shape[0]
    group = iota((devices, 2 * LANES), 1) % LANES // SUB
    both = join_cols(*parts(received))

    def members(r):
        line = jnp.broadcast_to(turned[CAP * SUB + r:CAP * SUB + r + 1], (NPATCH, devices))
        return (line == iota((NPATCH, devices), 0).astype(F32)).astype(BF16)

    def share(r):
        return jnp.where(group == r, both, jnp.zeros_like(both))

    gathered = fold(
        dot(join_cols(members(0), members(1)), join_rows(share(0), share(1))) + dot(members(2), share(2))
    )
    prior_high, prior_low = parts(prior_ref[...])
    high, low = parts(gathered)
    mixed = fold(dot(prior_high, join_cols(high, low))) + dot(prior_low, high)
    sub = join_cols(*[sub_ref[...]] * 4)
    sub_high, sub_low = parts(join_rows(*[sub] * CAP, jnp.zeros_like(sub)))
    high, low = parts(mixed)
    smoothed = dot(join_cols(high, low), join_rows(sub_high, sub_high)) + dot(high, sub_low)
    both = join_cols(*parts(smoothed))
    group = iota((devices, LANES), 1) // SUB
    reply = None
    for r in range(CAP):
        line = jnp.broadcast_to(received[:, CAP * SUB + r:CAP * SUB + r + 1], (devices, NPATCH))
        member = (line == iota((devices, NPATCH), 1).astype(F32)).astype(BF16)
        found = fold(dot(member, both))
        reply = found if reply is None else jnp.where(group == r, found, reply)
    reply_ref[...] = reply
    write.wait()


def backward(ret_ref, hot_t_ref, mask_ref, lat4_ref, lon_ref, out_ref, buf, sems):
    mask = mask_ref[...]
    picked = dot(hot_t_ref[...], join_rows(*parts(ret_ref[...])))
    picked = jnp.where(iota(mask.shape, 1) < CAP * SUB, picked * mask, 0.0)
    picked = picked + pltpu.roll(picked, 2 * SUB, 1)
    picked = picked + pltpu.roll(picked, SUB, 1)
    rows = buf.shape[0]
    tile_rows = rows // TS
    group = iota((tile_rows, LANES), 1) // SUB
    halves = []
    for q in range(2):
        half = picked[4 * q * tile_rows:(4 * q + 1) * tile_rows]
        for g in range(1, 4):
            block = picked[(4 * q + g) * tile_rows:(4 * q + g + 1) * tile_rows]
            half = jnp.where(group == g, block, half)
        halves.append(half)
    value = join_cols(*halves)
    lon = lon_ref[...]
    writes = []
    share = rows // WRITES
    for i in range(WRITES):
        part = value[i * share // TS:(i + 1) * share // TS]
        wide = jnp.broadcast_to(part[:, None, :], (share // TS, TS, part.shape[1]))
        lat4 = lat4_ref[i * share:(i + 1) * share, :]
        high, low = parts(wide.reshape(share, part.shape[1]) * join_cols(lat4, lat4))
        buf[i * share:(i + 1) * share, :] = fold(dot(high, lon)) + dot(low, lon[:, :LANES])
        span = pl.ds(i * share, share)
        writes.append(pltpu.make_async_copy(buf.at[span], out_ref.at[span], sems.at[i]))
        writes[-1].start()
    for write in writes:
        write.wait()


VMEM = pl.BlockSpec(memory_space=pltpu.VMEM)
HBM = pl.BlockSpec(memory_space=pltpu.HBM)


def call(kernel, ins, outs, *args, scratch=()):
    return pl.pallas_call(
        kernel,
        out_shape=[jax.ShapeDtypeStruct(shape, dtype) for shape, dtype, _ in outs],
        in_specs=ins,
        out_specs=[spec for _, _, spec in outs],
        scratch_shapes=scratch,
        compiler_params=pltpu.CompilerParams(vmem_limit_bytes=32 * 1024 * 1024),
    )(*args)


def swap_pairs(axis, first, periodic):
    count = lax.axis_size(axis)
    pairs = []
    for a in range(first, count, 2):
        b = a + 1
        if b == count:
            if not periodic:
                continue
            b = 0
        pairs += [(a, b), (b, a)]
    return pairs


def swap(payload, axis, periodic):
    far, _ = lax.optimization_barrier((payload[1], payload[0]))
    far = lax.ppermute(far, axis, swap_pairs(axis, 1, periodic))
    return lax.ppermute(payload[0], axis, swap_pairs(axis, 0, periodic)), far


def local(
    adjoint_height,
    depth,
    wet,
    basis_lat,
    basis_lon,
    tile_owner,
    tile_patch,
    tile_count,
    prior_patches,
    prior_subfaults,
):
    rows, cols = adjoint_height.shape
    lon_devices = lax.axis_size("lon")
    total = (rows // TS) * (cols // TS)

    def edge_rows(start):
        def cut(x):
            return lax.dynamic_slice_in_dim(x, start, 8, axis=0)
        return jnp.concatenate([cut(adjoint_height), cut(depth) * cut(wet).astype(F32)], axis=0)

    last = (rows - 8) * (1 - (lax.axis_index("lat") & 1))
    north_a, north_b = swap([edge_rows(last), edge_rows(rows - 8 - last)], "lat", False)
    dma = pltpu.SemaphoreType.DMA
    own = pltpu.VMEM((rows, cols), F32)
    tile_shape = (cols // TS, rows // TS)
    resident = [
        basis_lat, basis_lon, tile_owner.T, tile_patch.T, tile_count.T, adjoint_height, depth, wet
    ]
    height, wet_depth, edges, lat4, lon, lon_t, hot, hot_t, mask = call(
        prepare,
        [HBM] * len(resident),
        [
            ((rows, cols), F32, VMEM),
            ((rows, cols), F32, VMEM),
            ((4 * EDGE, rows), F32, VMEM),
            ((rows, LANES), F32, VMEM),
            ((total, 2 * LANES), BF16, VMEM),
            ((2 * LANES, total), BF16, VMEM),
            ((lon_devices, total), BF16, VMEM),
            ((total, 2 * lon_devices), BF16, VMEM),
            ((total, LANES), F32, VMEM),
        ],
        *[pltpu.with_memory_space_constraint(x, pltpu.HBM) for x in resident],
        scratch=[pltpu.VMEM((SUB, rows), F32), pltpu.VMEM((SUB, cols), F32)]
        + [pltpu.VMEM(tile_shape, jnp.int32)] * 3
        + [own, pltpu.VMEM((rows, cols), jnp.int32), dma((len(resident),))],
    )
    payload = ((2 * RIM, rows + LANES), F32, VMEM)
    first, second, block = call(
        corners,
        [VMEM] * 3,
        [payload, payload, ((4 * EDGE, LANES), F32, VMEM)],
        edges, north_a, north_b,
    )
    east_a, east_b = swap([first, second], "lon", True)
    (middle,) = call(
        inner, [VMEM] * 4, [((rows, cols), F32, VMEM)],
        height, wet_depth, north_a, north_b,
    )
    ended, sent = call(
        forward,
        [VMEM] * 9,
        [((rows, cols), F32, VMEM), ((lon_devices, LANES), F32, VMEM)],
        middle, edges, block, east_a, east_b, lat4, lon_t, hot, mask,
    )
    received = lax.all_to_all(sent, "lon", split_axis=0, concat_axis=0, tiled=True)
    replies, final = call(
        smooth,
        [VMEM] * 4,
        [((lon_devices, LANES), F32, VMEM), ((rows, cols), F32, HBM)],
        received, prior_patches.reshape(NPATCH, NPATCH), prior_subfaults, ended,
        scratch=[dma(())],
    )
    returned = lax.all_to_all(replies, "lon", split_axis=0, concat_axis=0, tiled=True)
    (gradient,) = call(
        backward,
        [VMEM] * 5,
        [((rows, cols), F32, HBM)],
        returned, hot_t, mask, lat4, lon,
        scratch=[own, dma((WRITES,))],
    )
    return (final, gradient)


def solution(mesh):
    return jax.shard_map(
        local,
        mesh=mesh,
        in_specs=(
            P("lat", "lon"),
            P("lat", "lon"),
            P("lat", "lon"),
            P(None, "lat"),
            P(None, "lon"),
            P("lat", "lon"),
            P("lat", "lon"),
            P("lat", "lon"),
            P("lat", "lon", None, None),
            P(),
        ),
        out_specs=(P("lat", "lon"), P("lat", "lon")),
        check_vma=False,
    )
```

```python
import jax
import jax.numpy as jnp
from jax import lax
from jax.experimental import pallas as pl
from jax.experimental.pallas import tpu as pltpu
from jax.sharding import PartitionSpec as P

STEPS = 4
RIM = 4
TS = 16
SUB = 32
NPATCH = 256
CAP = 3
EDGE = 8
WRITES = 2
CHUNKS = 4
COURANT = 0.6
LANES = 128
F32 = jnp.float32
BF16 = jnp.bfloat16


def iota(shape, dim):
    return lax.broadcasted_iota(jnp.int32, shape, dim)


def parts(x):
    high = x.astype(BF16)
    return high, (x - high.astype(F32)).astype(BF16)


def dot(a, b):
    return lax.dot_general(a, b, (((1,), (0,)), ((), ())), preferred_element_type=F32)


def join_cols(*blocks):
    return jnp.concatenate(blocks, axis=1)


def join_rows(*blocks):
    return jnp.concatenate(blocks, axis=0)


def fold(x):
    return x[:, :LANES] + x[:, LANES:]


def spread_lon(basis_lon):
    tiles = LANES // TS
    tall = join_rows(*[basis_lon] * tiles)
    inside = iota(tall.shape, 0) // SUB == iota(tall.shape, 1) // TS
    return jnp.where(inside, tall, 0.0)


def edge_columns(height, wet_depth):
    lane = iota(height.shape, 1)
    near = jnp.where(lane < EDGE, height, pltpu.roll(wet_depth, EDGE, 1))
    far = jnp.where(lane >= LANES - EDGE, height, pltpu.roll(wet_depth, LANES - EDGE, 1))
    return jnp.where(lane < LANES // 2, near, far)


def pick_edges(turned):
    return join_rows(turned[0:2 * EDGE], turned[LANES - 2 * EDGE:])


def prepare(lat_hbm, lon_hbm, owner_hbm, patch_hbm, count_hbm, h_hbm, d_hbm, w_hbm,
            height_ref, wet_depth_ref, edge_ref, lat4_ref, lon_ref, lon_t_ref, hot_ref, hot_t_ref,
            mask_ref, lat_buf, lon_buf, owner_buf, patch_buf, count_buf, depth_buf, wet_buf, sems):
    pairs = [(lat_hbm, lat_buf), (lon_hbm, lon_buf), (owner_hbm, owner_buf), (patch_hbm, patch_buf),
             (count_hbm, count_buf), (h_hbm, height_ref), (d_hbm, depth_buf), (w_hbm, wet_buf)]
    copies = [pltpu.make_async_copy(src, dst, sems.at[i]) for i, (src, dst) in enumerate(pairs)]
    for copy in copies:
        copy.start()
    for copy in copies[:5]:
        copy.wait()
    lat4_ref[...] = join_rows(*[lat_buf[...]] * 4).T
    spread = spread_lon(lon_buf[...])
    lon_ref[...] = join_cols(*parts(spread))
    lon_t_ref[...] = join_rows(*parts(spread.T))

    def column(ref):
        table = ref[...].astype(F32).T
        flat = join_rows(*[table[:, k:k + 1] for k in range(table.shape[1])])
        return jnp.broadcast_to(flat, (flat.shape[0], LANES))

    owner = column(owner_buf)
    patch = column(patch_buf)
    count = column(count_buf)
    owner_row = owner.T
    total = owner.shape[0]
    hot_t = (owner == iota(owner.shape, 1).astype(F32)).astype(BF16)
    hot_t_ref[...] = join_cols(hot_t, hot_t)
    hot_ref[...] = (owner_row == iota(owner_row.shape, 0).astype(F32)).astype(BF16)
    rank = jnp.zeros((total, LANES), F32)
    for q in range(total // LANES):
        row = jnp.broadcast_to(owner_row[0:1, q * LANES:(q + 1) * LANES], (total, LANES))
        earlier = iota((total, LANES), 1) + q * LANES < iota((total, LANES), 0)
        rank = rank + jnp.where(earlier & (row == owner), 1.0, 0.0)
    rank = jnp.broadcast_to(jnp.sum(rank, axis=1, keepdims=True), (total, LANES))
    lane = iota((total, LANES), 1)
    group = (lane // SUB).astype(F32)
    place = (lane % SUB).astype(F32)
    live = jnp.where((rank == group) & (place < count), 1.0, 0.0)
    number = jnp.where(rank == place, patch, 0.0)
    mask_ref[...] = jnp.where(lane < CAP * SUB, live, number)

    for copy in copies[5:]:
        copy.wait()
    wet_depth = depth_buf[...] * wet_buf[...].astype(F32)
    wet_depth_ref[...] = wet_depth
    edge_ref[...] = pick_edges(edge_columns(height_ref[...], wet_depth).T)


def is_even(axis):
    return (lax.axis_index(axis) & 1) == 0


def rims(ra, rb):
    even = is_even("lat")
    return jnp.where(even, rb, ra), jnp.where(even, ra, rb)


def corners(edge_ref, ra_ref, rb_ref, first_ref, second_ref, block_ref):
    north, south = rims(ra_ref[...], rb_ref[...])
    block = join_rows(
        edge_columns(south[0:8], south[8:16]),
        jnp.zeros((LANES - 16, LANES), F32),
        edge_columns(north[0:8], north[8:16]),
    ).T
    block = pick_edges(block)
    block_ref[...] = block
    strips = join_cols(edge_ref[...], block)
    west = join_rows(strips[0:RIM], strips[EDGE:EDGE + RIM])
    east = join_rows(strips[4 * EDGE - RIM:], strips[3 * EDGE - RIM:3 * EDGE])
    even = is_even("lon")
    first_ref[...] = jnp.where(even, east, west)
    second_ref[...] = jnp.where(even, west, east)


def march(height, wet_depth, right, below):
    def ahead(x, dim):
        return pltpu.roll(x, x.shape[dim] - 1, dim)

    ce = COURANT * jnp.minimum(wet_depth, ahead(wet_depth, right))
    cn = COURANT * jnp.minimum(wet_depth, ahead(wet_depth, below))
    east = jnp.zeros_like(height)
    north = jnp.zeros_like(height)
    for _ in range(STEPS):
        east = east + ce * (ahead(height, right) - height)
        north = north + cn * (ahead(height, below) - height)
        height = (
            height
            + COURANT * (east - pltpu.roll(east, 1, right))
            + COURANT * (north - pltpu.roll(north, 1, below))
        )
    return height


def inner(height_ref, wet_depth_ref, ra_ref, rb_ref, out_ref):
    north, south = rims(ra_ref[...], rb_ref[...])
    height = join_rows(north[0:8], height_ref[...], south[0:8])
    wet_depth = join_rows(north[8:16], wet_depth_ref[...], south[8:16])
    out_ref[...] = march(height, wet_depth, 1, 0)[8:8 + out_ref.shape[0]]


def forward(inner_ref, edge_ref, block_ref, ea_ref, eb_ref, lat4_ref, lon_t_ref,
            hot_ref, mask_ref, final_ref, send_ref):
    rows_own = inner_ref.shape[0]
    even = is_even("lon")
    from_east = jnp.where(even, ea_ref[...], eb_ref[...])
    from_west = jnp.where(even, eb_ref[...], ea_ref[...])
    own = join_cols(edge_ref[...], block_ref[...])
    strip = march(
        join_rows(from_west[0:RIM], own[0:EDGE], own[3 * EDGE:], from_east[0:RIM]),
        join_rows(from_west[RIM:], own[EDGE:2 * EDGE], own[2 * EDGE:3 * EDGE], from_east[RIM:]),
        0, 1,
    )[:, :rows_own]
    table = join_rows(
        strip[RIM:2 * RIM], jnp.zeros((LANES - 2 * RIM, rows_own), F32), strip[2 * EDGE:2 * EDGE + RIM]
    ).T
    lon_high, lon_low = lon_t_ref[:LANES, :], lon_t_ref[LANES:, :]
    lon_both = join_rows(lon_high, lon_high)
    tile_rows = rows_own // TS
    share = rows_own // CHUNKS
    lane = iota((share, LANES), 1)
    pieces = []
    for i in range(CHUNKS):
        span = slice(i * share, (i + 1) * share)
        final = jnp.where((lane < RIM) | (lane >= LANES - RIM), table[span], inner_ref[span, :])
        final_ref[span, :] = final
        high, low = parts(final)
        lat4 = lat4_ref[span, :]
        product = (dot(join_cols(high, low), lon_both) + dot(high, lon_low)) * join_cols(lat4, lat4)
        pieces.append(jnp.sum(product.reshape(share // TS, TS, product.shape[1]), axis=1))
    sums = join_rows(*pieces)
    group = iota((tile_rows, LANES), 1) // SUB
    stacked = []
    for q in range(sums.shape[1] // LANES):
        for g in range(4):
            part = jnp.where(group == g, sums[:, q * LANES:(q + 1) * LANES], 0.0)
            part = part + pltpu.roll(part, 2 * SUB, 1)
            stacked.append(part + pltpu.roll(part, SUB, 1))
    values = join_rows(*stacked)
    mask = mask_ref[...]
    filled = jnp.where(iota(mask.shape, 1) < CAP * SUB, values * mask, mask)
    send_ref[...] = fold(dot(hot_ref[...], join_cols(*parts(filled))))


def smooth(recv_ref, prior_ref, sub_ref, final_ref, reply_ref, out_ref, sem):
    write = pltpu.make_async_copy(final_ref, out_ref, sem)
    write.start()
    received = recv_ref[...]
    turned = received.T
    devices = received.shape[0]
    group = iota((devices, 2 * LANES), 1) % LANES // SUB
    both = join_cols(*parts(received))

    def members(r):
        line = jnp.broadcast_to(turned[CAP * SUB + r:CAP * SUB + r + 1], (NPATCH, devices))
        return (line == iota((NPATCH, devices), 0).astype(F32)).astype(BF16)

    def share(r):
        return jnp.where(group == r, both, jnp.zeros_like(both))

    gathered = fold(
        dot(join_cols(members(0), members(1)), join_rows(share(0), share(1))) + dot(members(2), share(2))
    )
    prior_high, prior_low = parts(prior_ref[...])
    high, low = parts(gathered)
    mixed = fold(dot(prior_high, join_cols(high, low))) + dot(prior_low, high)
    sub = join_cols(*[sub_ref[...]] * 4)
    sub_high, sub_low = parts(join_rows(*[sub] * CAP, jnp.zeros_like(sub)))
    high, low = parts(mixed)
    smoothed = dot(join_cols(high, low), join_rows(sub_high, sub_high)) + dot(high, sub_low)
    both = join_cols(*parts(smoothed))
    group = iota((devices, LANES), 1) // SUB
    reply = None
    for r in range(CAP):
        line = jnp.broadcast_to(received[:, CAP * SUB + r:CAP * SUB + r + 1], (devices, NPATCH))
        member = (line == iota((devices, NPATCH), 1).astype(F32)).astype(BF16)
        found = fold(dot(member, both))
        reply = found if reply is None else jnp.where(group == r, found, reply)
    reply_ref[...] = reply
    write.wait()


def backward(ret_ref, hot_t_ref, mask_ref, lat4_ref, lon_ref, out_ref, buf, sems):
    mask = mask_ref[...]
    picked = dot(hot_t_ref[...], join_rows(*parts(ret_ref[...])))
    picked = jnp.where(iota(mask.shape, 1) < CAP * SUB, picked * mask, 0.0)
    picked = picked + pltpu.roll(picked, 2 * SUB, 1)
    picked = picked + pltpu.roll(picked, SUB, 1)
    rows = buf.shape[0]
    tile_rows = rows // TS
    group = iota((tile_rows, LANES), 1) // SUB
    halves = []
    for q in range(2):
        half = picked[4 * q * tile_rows:(4 * q + 1) * tile_rows]
        for g in range(1, 4):
            block = picked[(4 * q + g) * tile_rows:(4 * q + g + 1) * tile_rows]
            half = jnp.where(group == g, block, half)
        halves.append(half)
    value = join_cols(*halves)
    lon = lon_ref[...]
    writes = []
    share = rows // WRITES
    for i in range(WRITES):
        part = value[i * share // TS:(i + 1) * share // TS]
        wide = jnp.broadcast_to(part[:, None, :], (share // TS, TS, part.shape[1]))
        lat4 = lat4_ref[i * share:(i + 1) * share, :]
        high, low = parts(wide.reshape(share, part.shape[1]) * join_cols(lat4, lat4))
        buf[i * share:(i + 1) * share, :] = fold(dot(high, lon)) + dot(low, lon[:, :LANES])
        span = pl.ds(i * share, share)
        writes.append(pltpu.make_async_copy(buf.at[span], out_ref.at[span], sems.at[i]))
        writes[-1].start()
    for write in writes:
        write.wait()


VMEM = pl.BlockSpec(memory_space=pltpu.VMEM)
HBM = pl.BlockSpec(memory_space=pltpu.HBM)


def call(kernel, ins, outs, *args, scratch=()):
    return pl.pallas_call(
        kernel,
        out_shape=[jax.ShapeDtypeStruct(shape, dtype) for shape, dtype, _ in outs],
        in_specs=ins,
        out_specs=[spec for _, _, spec in outs],
        scratch_shapes=scratch,
        compiler_params=pltpu.CompilerParams(vmem_limit_bytes=32 * 1024 * 1024),
    )(*args)


def swap_pairs(axis, first, periodic):
    count = lax.axis_size(axis)
    pairs = []
    for a in range(first, count, 2):
        b = a + 1
        if b == count:
            if not periodic:
                continue
            b = 0
        pairs += [(a, b), (b, a)]
    return pairs


def swap(payload, axis, periodic):
    far, _ = lax.optimization_barrier((payload[1], payload[0]))
    far = lax.ppermute(far, axis, swap_pairs(axis, 1, periodic))
    return lax.ppermute(payload[0], axis, swap_pairs(axis, 0, periodic)), far


def local(
    adjoint_height,
    depth,
    wet,
    basis_lat,
    basis_lon,
    tile_owner,
    tile_patch,
    tile_count,
    prior_patches,
    prior_subfaults,
):
    rows, cols = adjoint_height.shape
    lon_devices = lax.axis_size("lon")
    total = (rows // TS) * (cols // TS)

    def edge_rows(start):
        def cut(x):
            return lax.dynamic_slice_in_dim(x, start, 8, axis=0)
        return jnp.concatenate([cut(adjoint_height), cut(depth) * cut(wet).astype(F32)], axis=0)

    last = (rows - 8) * (1 - (lax.axis_index("lat") & 1))
    north_a, north_b = swap([edge_rows(last), edge_rows(rows - 8 - last)], "lat", False)
    dma = pltpu.SemaphoreType.DMA
    own = pltpu.VMEM((rows, cols), F32)
    tile_shape = (cols // TS, rows // TS)
    resident = [
        basis_lat, basis_lon, tile_owner.T, tile_patch.T, tile_count.T, adjoint_height, depth, wet
    ]
    height, wet_depth, edges, lat4, lon, lon_t, hot, hot_t, mask = call(
        prepare,
        [HBM] * len(resident),
        [
            ((rows, cols), F32, VMEM),
            ((rows, cols), F32, VMEM),
            ((4 * EDGE, rows), F32, VMEM),
            ((rows, LANES), F32, VMEM),
            ((total, 2 * LANES), BF16, VMEM),
            ((2 * LANES, total), BF16, VMEM),
            ((lon_devices, total), BF16, VMEM),
            ((total, 2 * lon_devices), BF16, VMEM),
            ((total, LANES), F32, VMEM),
        ],
        *[pltpu.with_memory_space_constraint(x, pltpu.HBM) for x in resident],
        scratch=[pltpu.VMEM((SUB, rows), F32), pltpu.VMEM((SUB, cols), F32)]
        + [pltpu.VMEM(tile_shape, jnp.int32)] * 3
        + [own, pltpu.VMEM((rows, cols), jnp.int32), dma((len(resident),))],
    )
    payload = ((2 * RIM, rows + LANES), F32, VMEM)
    first, second, block = call(
        corners,
        [VMEM] * 3,
        [payload, payload, ((4 * EDGE, LANES), F32, VMEM)],
        edges, north_a, north_b,
    )
    east_a, east_b = swap([first, second], "lon", True)
    (middle,) = call(
        inner, [VMEM] * 4, [((rows, cols), F32, VMEM)],
        height, wet_depth, north_a, north_b,
    )
    ended, sent = call(
        forward,
        [VMEM] * 9,
        [((rows, cols), F32, VMEM), ((lon_devices, LANES), F32, VMEM)],
        middle, edges, block, east_a, east_b, lat4, lon_t, hot, mask,
    )
    received = lax.all_to_all(sent, "lon", split_axis=0, concat_axis=0, tiled=True)
    replies, final = call(
        smooth,
        [VMEM] * 4,
        [((lon_devices, LANES), F32, VMEM), ((rows, cols), F32, HBM)],
        received, prior_patches.reshape(NPATCH, NPATCH), prior_subfaults, ended,
        scratch=[dma(())],
    )
    returned = lax.all_to_all(replies, "lon", split_axis=0, concat_axis=0, tiled=True)
    (gradient,) = call(
        backward,
        [VMEM] * 5,
        [((rows, cols), F32, HBM)],
        returned, hot_t, mask, lat4, lon,
        scratch=[own, dma((WRITES,))],
    )
    return (final, gradient)


def solution(mesh):
    return jax.shard_map(
        local,
        mesh=mesh,
        in_specs=(
            P("lat", "lon"),
            P("lat", "lon"),
            P("lat", "lon"),
            P(None, "lat"),
            P(None, "lon"),
            P("lat", "lon"),
            P("lat", "lon"),
            P("lat", "lon"),
            P("lat", "lon", None, None),
            P(),
        ),
        out_specs=(P("lat", "lon"), P("lat", "lon")),
        check_vma=False,
    )
```

```python
import jax
import jax.numpy as jnp
from jax import lax
from jax.experimental import pallas as pl
from jax.experimental.pallas import tpu as pltpu
from jax.sharding import PartitionSpec as P

STEPS = 4
RIM = 4
TS = 16
SUB = 32
NPATCH = 256
CAP = 3
EDGE = 8
WRITES = 2
CHUNKS = 4
COURANT = 0.6
LANES = 128
F32 = jnp.float32
BF16 = jnp.bfloat16


def iota(shape, dim):
    return lax.broadcasted_iota(jnp.int32, shape, dim)


def parts(x):
    high = x.astype(BF16)
    return high, (x - high.astype(F32)).astype(BF16)


def dot(a, b):
    return lax.dot_general(a, b, (((1,), (0,)), ((), ())), preferred_element_type=F32)


def join_cols(*blocks):
    return jnp.concatenate(blocks, axis=1)


def join_rows(*blocks):
    return jnp.concatenate(blocks, axis=0)


def fold(x):
    return x[:, :LANES] + x[:, LANES:]


def spread_lon(basis_lon):
    tiles = LANES // TS
    tall = join_rows(*[basis_lon] * tiles)
    inside = iota(tall.shape, 0) // SUB == iota(tall.shape, 1) // TS
    return jnp.where(inside, tall, 0.0)


def edge_columns(height, wet_depth):
    lane = iota(height.shape, 1)
    near = jnp.where(lane < EDGE, height, pltpu.roll(wet_depth, EDGE, 1))
    far = jnp.where(lane >= LANES - EDGE, height, pltpu.roll(wet_depth, LANES - EDGE, 1))
    return jnp.where(lane < LANES // 2, near, far)


def pick_edges(turned):
    return join_rows(turned[0:2 * EDGE], turned[LANES - 2 * EDGE:])


def prepare(lat_hbm, lon_hbm, owner_hbm, patch_hbm, count_hbm, h_hbm, d_hbm, w_hbm,
            height_ref, wet_depth_ref, edge_ref, lat4_ref, lon_ref, lon_t_ref, hot_ref, hot_t_ref,
            mask_ref, lat_buf, lon_buf, owner_buf, patch_buf, count_buf, depth_buf, wet_buf, sems):
    pairs = [(lat_hbm, lat_buf), (lon_hbm, lon_buf), (owner_hbm, owner_buf), (patch_hbm, patch_buf),
             (count_hbm, count_buf), (h_hbm, height_ref), (d_hbm, depth_buf), (w_hbm, wet_buf)]
    copies = [pltpu.make_async_copy(src, dst, sems.at[i]) for i, (src, dst) in enumerate(pairs)]
    for copy in copies:
        copy.start()
    for copy in copies[:5]:
        copy.wait()
    lat4_ref[...] = join_rows(*[lat_buf[...]] * 4).T
    spread = spread_lon(lon_buf[...])
    lon_ref[...] = join_cols(*parts(spread))
    lon_t_ref[...] = join_rows(*parts(spread.T))

    def column(ref):
        table = ref[...].astype(F32).T
        flat = join_rows(*[table[:, k:k + 1] for k in range(table.shape[1])])
        return jnp.broadcast_to(flat, (flat.shape[0], LANES))

    owner = column(owner_buf)
    patch = column(patch_buf)
    count = column(count_buf)
    owner_row = owner.T
    total = owner.shape[0]
    hot_t = (owner == iota(owner.shape, 1).astype(F32)).astype(BF16)
    hot_t_ref[...] = join_cols(hot_t, hot_t)
    hot_ref[...] = (owner_row == iota(owner_row.shape, 0).astype(F32)).astype(BF16)
    rank = jnp.zeros((total, LANES), F32)
    for q in range(total // LANES):
        row = jnp.broadcast_to(owner_row[0:1, q * LANES:(q + 1) * LANES], (total, LANES))
        earlier = iota((total, LANES), 1) + q * LANES < iota((total, LANES), 0)
        rank = rank + jnp.where(earlier & (row == owner), 1.0, 0.0)
    rank = jnp.broadcast_to(jnp.sum(rank, axis=1, keepdims=True), (total, LANES))
    lane = iota((total, LANES), 1)
    group = (lane // SUB).astype(F32)
    place = (lane % SUB).astype(F32)
    live = jnp.where((rank == group) & (place < count), 1.0, 0.0)
    number = jnp.where(rank == place, patch, 0.0)
    mask_ref[...] = jnp.where(lane < CAP * SUB, live, number)

    for copy in copies[5:]:
        copy.wait()
    wet_depth = depth_buf[...] * wet_buf[...].astype(F32)
    wet_depth_ref[...] = wet_depth
    edge_ref[...] = pick_edges(edge_columns(height_ref[...], wet_depth).T)


def is_even(axis):
    return (lax.axis_index(axis) & 1) == 0


def rims(ra, rb):
    even = is_even("lat")
    return jnp.where(even, rb, ra), jnp.where(even, ra, rb)


def corners(edge_ref, ra_ref, rb_ref, first_ref, second_ref, block_ref):
    north, south = rims(ra_ref[...], rb_ref[...])
    block = join_rows(
        edge_columns(south[0:8], south[8:16]),
        jnp.zeros((LANES - 16, LANES), F32),
        edge_columns(north[0:8], north[8:16]),
    ).T
    block = pick_edges(block)
    block_ref[...] = block
    strips = join_cols(edge_ref[...], block)
    west = join_rows(strips[0:RIM], strips[EDGE:EDGE + RIM])
    east = join_rows(strips[4 * EDGE - RIM:], strips[3 * EDGE - RIM:3 * EDGE])
    even = is_even("lon")
    first_ref[...] = jnp.where(even, east, west)
    second_ref[...] = jnp.where(even, west, east)


def march(height, wet_depth, right, below):
    def ahead(x, dim):
        return pltpu.roll(x, x.shape[dim] - 1, dim)

    ce = COURANT * jnp.minimum(wet_depth, ahead(wet_depth, right))
    cn = COURANT * jnp.minimum(wet_depth, ahead(wet_depth, below))
    east = jnp.zeros_like(height)
    north = jnp.zeros_like(height)
    for _ in range(STEPS):
        east = east + ce * (ahead(height, right) - height)
        north = north + cn * (ahead(height, below) - height)
        height = (
            height
            + COURANT * (east - pltpu.roll(east, 1, right))
            + COURANT * (north - pltpu.roll(north, 1, below))
        )
    return height


def inner(height_ref, wet_depth_ref, ra_ref, rb_ref, out_ref):
    north, south = rims(ra_ref[...], rb_ref[...])
    height = join_rows(north[0:8], height_ref[...], south[0:8])
    wet_depth = join_rows(north[8:16], wet_depth_ref[...], south[8:16])
    out_ref[...] = march(height, wet_depth, 1, 0)[8:8 + out_ref.shape[0]]


def forward(inner_ref, edge_ref, block_ref, ea_ref, eb_ref, lat4_ref, lon_t_ref,
            hot_ref, mask_ref, final_ref, send_ref):
    rows_own = inner_ref.shape[0]
    even = is_even("lon")
    from_east = jnp.where(even, ea_ref[...], eb_ref[...])
    from_west = jnp.where(even, eb_ref[...], ea_ref[...])
    own = join_cols(edge_ref[...], block_ref[...])
    strip = march(
        join_rows(from_west[0:RIM], own[0:EDGE], own[3 * EDGE:], from_east[0:RIM]),
        join_rows(from_west[RIM:], own[EDGE:2 * EDGE], own[2 * EDGE:3 * EDGE], from_east[RIM:]),
        0, 1,
    )[:, :rows_own]
    table = join_rows(
        strip[RIM:2 * RIM], jnp.zeros((LANES - 2 * RIM, rows_own), F32), strip[2 * EDGE:2 * EDGE + RIM]
    ).T
    lon_high, lon_low = lon_t_ref[:LANES, :], lon_t_ref[LANES:, :]
    lon_both = join_rows(lon_high, lon_high)
    tile_rows = rows_own // TS
    share = rows_own // CHUNKS
    lane = iota((share, LANES), 1)
    pieces = []
    for i in range(CHUNKS):
        span = slice(i * share, (i + 1) * share)
        final = jnp.where((lane < RIM) | (lane >= LANES - RIM), table[span], inner_ref[span, :])
        final_ref[span, :] = final
        high, low = parts(final)
        lat4 = lat4_ref[span, :]
        product = (dot(join_cols(high, low), lon_both) + dot(high, lon_low)) * join_cols(lat4, lat4)
        pieces.append(jnp.sum(product.reshape(share // TS, TS, product.shape[1]), axis=1))
    sums = join_rows(*pieces)
    group = iota((tile_rows, LANES), 1) // SUB
    stacked = []
    for q in range(sums.shape[1] // LANES):
        for g in range(4):
            part = jnp.where(group == g, sums[:, q * LANES:(q + 1) * LANES], 0.0)
            part = part + pltpu.roll(part, 2 * SUB, 1)
            stacked.append(part + pltpu.roll(part, SUB, 1))
    values = join_rows(*stacked)
    mask = mask_ref[...]
    filled = jnp.where(iota(mask.shape, 1) < CAP * SUB, values * mask, mask)
    send_ref[...] = fold(dot(hot_ref[...], join_cols(*parts(filled))))


def smooth(recv_ref, prior_ref, sub_ref, final_ref, reply_ref, out_ref, sem):
    write = pltpu.make_async_copy(final_ref, out_ref, sem)
    write.start()
    received = recv_ref[...]
    turned = received.T
    devices = received.shape[0]
    group = iota((devices, 2 * LANES), 1) % LANES // SUB
    both = join_cols(*parts(received))

    def members(r):
        line = jnp.broadcast_to(turned[CAP * SUB + r:CAP * SUB + r + 1], (NPATCH, devices))
        return (line == iota((NPATCH, devices), 0).astype(F32)).astype(BF16)

    def share(r):
        return jnp.where(group == r, both, jnp.zeros_like(both))

    gathered = fold(
        dot(join_cols(members(0), members(1)), join_rows(share(0), share(1))) + dot(members(2), share(2))
    )
    prior_high, prior_low = parts(prior_ref[...])
    high, low = parts(gathered)
    mixed = fold(dot(prior_high, join_cols(high, low))) + dot(prior_low, high)
    sub = join_cols(*[sub_ref[...]] * 4)
    sub_high, sub_low = parts(join_rows(*[sub] * CAP, jnp.zeros_like(sub)))
    high, low = parts(mixed)
    smoothed = dot(join_cols(high, low), join_rows(sub_high, sub_high)) + dot(high, sub_low)
    both = join_cols(*parts(smoothed))
    group = iota((devices, LANES), 1) // SUB
    numbers = join_rows(*[
        jnp.broadcast_to(received[:, CAP * SUB + r:CAP * SUB + r + 1], (devices, NPATCH))
        for r in range(CAP)
    ])
    found = fold(dot((numbers == iota(numbers.shape, 1).astype(F32)).astype(BF16), both))
    reply = found[:devices]
    for r in range(1, CAP):
        reply = jnp.where(group == r, found[r * devices:(r + 1) * devices], reply)
    reply_ref[...] = reply
    write.wait()


def backward(ret_ref, hot_t_ref, mask_ref, lat4_ref, lon_ref, out_ref, buf, sems):
    mask = mask_ref[...]
    picked = dot(hot_t_ref[...], join_rows(*parts(ret_ref[...])))
    picked = jnp.where(iota(mask.shape, 1) < CAP * SUB, picked * mask, 0.0)
    picked = picked + pltpu.roll(picked, 2 * SUB, 1)
    picked = picked + pltpu.roll(picked, SUB, 1)
    rows = buf.shape[0]
    tile_rows = rows // TS
    group = iota((tile_rows, LANES), 1) // SUB
    halves = []
    for q in range(2):
        half = picked[4 * q * tile_rows:(4 * q + 1) * tile_rows]
        for g in range(1, 4):
            block = picked[(4 * q + g) * tile_rows:(4 * q + g + 1) * tile_rows]
            half = jnp.where(group == g, block, half)
        halves.append(half)
    value = join_cols(*halves)
    lon = lon_ref[...]
    writes = []
    share = rows // WRITES
    for i in range(WRITES):
        part = value[i * share // TS:(i + 1) * share // TS]
        wide = jnp.broadcast_to(part[:, None, :], (share // TS, TS, part.shape[1]))
        lat4 = lat4_ref[i * share:(i + 1) * share, :]
        high, low = parts(wide.reshape(share, part.shape[1]) * join_cols(lat4, lat4))
        buf[i * share:(i + 1) * share, :] = fold(dot(high, lon)) + dot(low, lon[:, :LANES])
        span = pl.ds(i * share, share)
        writes.append(pltpu.make_async_copy(buf.at[span], out_ref.at[span], sems.at[i]))
        writes[-1].start()
    for write in writes:
        write.wait()


VMEM = pl.BlockSpec(memory_space=pltpu.VMEM)
HBM = pl.BlockSpec(memory_space=pltpu.HBM)


def call(kernel, ins, outs, *args, scratch=()):
    return pl.pallas_call(
        kernel,
        out_shape=[jax.ShapeDtypeStruct(shape, dtype) for shape, dtype, _ in outs],
        in_specs=ins,
        out_specs=[spec for _, _, spec in outs],
        scratch_shapes=scratch,
        compiler_params=pltpu.CompilerParams(vmem_limit_bytes=32 * 1024 * 1024),
    )(*args)


def swap_pairs(axis, first, periodic):
    count = lax.axis_size(axis)
    pairs = []
    for a in range(first, count, 2):
        b = a + 1
        if b == count:
            if not periodic:
                continue
            b = 0
        pairs += [(a, b), (b, a)]
    return pairs


def swap(payload, axis, periodic):
    far, _ = lax.optimization_barrier((payload[1], payload[0]))
    far = lax.ppermute(far, axis, swap_pairs(axis, 1, periodic))
    return lax.ppermute(payload[0], axis, swap_pairs(axis, 0, periodic)), far


def local(
    adjoint_height,
    depth,
    wet,
    basis_lat,
    basis_lon,
    tile_owner,
    tile_patch,
    tile_count,
    prior_patches,
    prior_subfaults,
):
    rows, cols = adjoint_height.shape
    lon_devices = lax.axis_size("lon")
    total = (rows // TS) * (cols // TS)

    def edge_rows(start):
        def cut(x):
            return lax.dynamic_slice_in_dim(x, start, 8, axis=0)
        return jnp.concatenate([cut(adjoint_height), cut(depth) * cut(wet).astype(F32)], axis=0)

    last = (rows - 8) * (1 - (lax.axis_index("lat") & 1))
    north_a, north_b = swap([edge_rows(last), edge_rows(rows - 8 - last)], "lat", False)
    dma = pltpu.SemaphoreType.DMA
    own = pltpu.VMEM((rows, cols), F32)
    tile_shape = (cols // TS, rows // TS)
    resident = [
        basis_lat, basis_lon, tile_owner.T, tile_patch.T, tile_count.T, adjoint_height, depth, wet
    ]
    height, wet_depth, edges, lat4, lon, lon_t, hot, hot_t, mask = call(
        prepare,
        [HBM] * len(resident),
        [
            ((rows, cols), F32, VMEM),
            ((rows, cols), F32, VMEM),
            ((4 * EDGE, rows), F32, VMEM),
            ((rows, LANES), F32, VMEM),
            ((total, 2 * LANES), BF16, VMEM),
            ((2 * LANES, total), BF16, VMEM),
            ((lon_devices, total), BF16, VMEM),
            ((total, 2 * lon_devices), BF16, VMEM),
            ((total, LANES), F32, VMEM),
        ],
        *[pltpu.with_memory_space_constraint(x, pltpu.HBM) for x in resident],
        scratch=[pltpu.VMEM((SUB, rows), F32), pltpu.VMEM((SUB, cols), F32)]
        + [pltpu.VMEM(tile_shape, jnp.int32)] * 3
        + [own, pltpu.VMEM((rows, cols), jnp.int32), dma((len(resident),))],
    )
    payload = ((2 * RIM, rows + LANES), F32, VMEM)
    first, second, block = call(
        corners,
        [VMEM] * 3,
        [payload, payload, ((4 * EDGE, LANES), F32, VMEM)],
        edges, north_a, north_b,
    )
    east_a, east_b = swap([first, second], "lon", True)
    (middle,) = call(
        inner, [VMEM] * 4, [((rows, cols), F32, VMEM)],
        height, wet_depth, north_a, north_b,
    )
    ended, sent = call(
        forward,
        [VMEM] * 9,
        [((rows, cols), F32, VMEM), ((lon_devices, LANES), F32, VMEM)],
        middle, edges, block, east_a, east_b, lat4, lon_t, hot, mask,
    )
    received = lax.all_to_all(sent, "lon", split_axis=0, concat_axis=0, tiled=True)
    replies, final = call(
        smooth,
        [VMEM] * 4,
        [((lon_devices, LANES), F32, VMEM), ((rows, cols), F32, HBM)],
        received, prior_patches.reshape(NPATCH, NPATCH), prior_subfaults, ended,
        scratch=[dma(())],
    )
    returned = lax.all_to_all(replies, "lon", split_axis=0, concat_axis=0, tiled=True)
    (gradient,) = call(
        backward,
        [VMEM] * 5,
        [((rows, cols), F32, HBM)],
        returned, hot_t, mask, lat4, lon,
        scratch=[own, dma((WRITES,))],
    )
    return (final, gradient)


def solution(mesh):
    return jax.shard_map(
        local,
        mesh=mesh,
        in_specs=(
            P("lat", "lon"),
            P("lat", "lon"),
            P("lat", "lon"),
            P(None, "lat"),
            P(None, "lon"),
            P("lat", "lon"),
            P("lat", "lon"),
            P("lat", "lon"),
            P("lat", "lon", None, None),
            P(),
        ),
        out_specs=(P("lat", "lon"), P("lat", "lon")),
        check_vma=False,
    )
```
